32 devices in a mesh: row: 4 (over y, core), col: 8 (over z, x).
Axes of the slice: x: 2, y: 2, z: 4, core: 2. Of those that a mesh axis runs over, the one named last changes fastest.
Arguments:
- pixels: bfloat16 [128, 256, 588], P('row', 'col'), may hold values from -6 to 6
- text: bfloat16 [12288, 1024], P(('row', 'col')), may hold values from -6 to 6
- token_source: int32 [36864], P(('row', 'col')), may hold values from 0 to 1407, as said below
- example_ids: int32 [36864], P(('row', 'col')), may hold values from 0 to 95, as said below
- cotangent: bfloat16 [36864, 1024], P(('row', 'col')), may hold values from -6 to 6
- conv_weight: bfloat16 [588, 1664], P(None, ('row', 'col')), may hold values from -0.25 to 0.25
- conv_bias: bfloat16 [1664], P(('row', 'col')), may hold values from -3 to 3
- proj_weight: bfloat16 [1664, 1024], P(None, ('row', 'col')), may hold values from -0.15625 to 0.15625
- proj_bias: bfloat16 [1024], P(('row', 'col')), may hold values from -3 to 3
- first_gain: bfloat16 [1024], P(('row', 'col')), may hold values from 0.099609375 to 1.8984375
- query_weight: bfloat16 [1024, 1024], P(('row', 'col')), may hold values from -0.1875 to 0.1875
- key_weight: bfloat16 [1024, 1024], P(('row', 'col')), may hold values from -0.1875 to 0.1875
- value_weight: bfloat16 [1024, 1024], P(('row', 'col')), may hold values from -0.1875 to 0.1875
- out_weight: bfloat16 [1024, 1024], P(None, ('row', 'col')), may hold values from -3 to 3
- second_gain: bfloat16 [1024], P(('row', 'col')), may hold values from 0.099609375 to 1.8984375
- gate_weight: bfloat16 [1024, 2816], P(('row', 'col')), may hold values from -0.1875 to 0.1875
- up_weight: bfloat16 [1024, 2816], P(('row', 'col')), may hold values from -0.1875 to 0.1875
- down_weight: bfloat16 [2816, 1024], P(None, ('row', 'col')), may hold values from -0.109375 to 0.109375
Outputs:
- output: bfloat16 [36864, 1024], P(('row', 'col'))
- pixel_grad: float32 [128, 256, 588], P('row', 'col')
- conv_weight_grad: float32 [588, 1664], P(None, ('row', 'col'))
- conv_bias_grad: float32 [1664], P(('row', 'col'))
- proj_weight_grad: float32 [1664, 1024], P(None, ('row', 'col'))
- proj_bias_grad: float32 [1024], P(('row', 'col'))
- first_gain_grad: float32 [1024], P(('row', 'col'))
- query_grad: float32 [1024, 1024], P(('row', 'col'))
- key_grad: float32 [1024, 1024], P(('row', 'col'))
- value_grad: float32 [1024, 1024], P(('row', 'col'))
- out_grad: float32 [1024, 1024], P(None, ('row', 'col'))
- second_gain_grad: float32 [1024], P(('row', 'col'))
- gate_grad: float32 [1024, 2816], P(('row', 'col'))
- up_grad: float32 [1024, 2816], P(('row', 'col'))
- down_grad: float32 [2816, 1024], P(None, ('row', 'col'))
The draws below stay inside these ranges and needn't reach their ends.
Inputs may be any that keep to these rules, and one draw needn't show every extreme that they name: `token_source`: within each packed row (tokens t with the same t div 1152) the sources are distinct; a row takes either all 1024 patch slots and text slots 1024 to 1151, or three quarters of its patch slots and all 384 text slots; slots that no token names are empty. `example_ids`: A packed row holds one example of 1152 tokens or three of 384 tokens each, every example contiguous and within one row; ids of different examples differ.
All inputs are finite; a program needn't handle non-finite values.
Results may differ from the reference program's by a relative error of at most 0.015.
Values may be sent and summed in bfloat16 or wider, within the bound.
No kernel may reach another device: no remote copies, remote signals or barrier semaphores. Data moves between devices by JAX's collectives and lax.ppermute only.
A program may use at most 256 MiB of HBM per device.

```python
import jax
import jax.numpy as jnp
from jax import lax

PD = 588
VW = 1664
D = 1024
H = 16
HD = 64
FF = 2816
PATCH_SLOTS = 1024
TEXT = 128
ROW = 1152
TILE_R = 32
TILE_C = 32
ROWS = 32
TOKENS = 36864
N_ROW = 4
N_COL = 8


def packed_layout(key):
    base = jax.random.fold_in(key, 7)
    kinds = jax.random.randint(jax.random.fold_in(base, 1), (ROWS,), 0, 2)
    row_index = jnp.arange(ROWS)
    kinds = jnp.where(row_index == 0, 1, jnp.where(row_index == ROWS - 1, 0, kinds))
    orders = jax.vmap(lambda part_key: jax.random.permutation(part_key, PATCH_SLOTS))(jax.random.split(jax.random.fold_in(base, 2), ROWS))
    position = jnp.arange(ROW)
    quarter = PATCH_SLOTS // 4
    span = quarter + TEXT
    example = position // span
    within = position % span
    small_patch = orders[:, jnp.minimum(example * quarter + within, PATCH_SLOTS - 1)]
    small_source = jnp.where(within[None, :] < quarter, small_patch, (PATCH_SLOTS + example * TEXT + within - quarter)[None, :])
    large_patch = orders[:, jnp.minimum(position, PATCH_SLOTS - 1)]
    large_source = jnp.where(position[None, :] < PATCH_SLOTS, large_patch, position[None, :])
    is_large = kinds[:, None] == 1
    source = jnp.where(is_large, large_source, small_source)
    idents = row_index[:, None] * 3 + jnp.where(is_large, 0, example[None, :])
    return (source.reshape(-1).astype(jnp.int32), idents.reshape(-1).astype(jnp.int32))


def draw_token_source(key, part):
    return packed_layout(key)[0]


def draw_example_ids(key, part):
    return packed_layout(key)[1]


def strengthened(array, key, source, target, blocks, factor):
    owner, partner = [(jnp.arange(array.shape[axis_at]) // (array.shape[axis_at] // blocks)).reshape([-1 if axis == axis_at else 1 for axis in range(array.ndim)]) for axis_at in (source, target)]
    chosen = jax.random.permutation(key, blocks)[partner]
    strong = (owner == chosen) | (owner == (partner + blocks // 2) % blocks)
    return jnp.where(strong, factor * array, array)


def level_of(key, shape, cuts, smallest, largest):
    def one(dim, blocks):
        draws = jax.random.uniform(jax.random.fold_in(jax.random.fold_in(key, 6), dim), (blocks,), jnp.float32, smallest / len(cuts), largest / len(cuts))
        return jnp.repeat(jnp.exp(draws), shape[dim] // blocks).reshape((-1,) + (1,) * (len(shape) - dim - 1))

    level = one(*cuts[0])
    for cut in cuts[1:]:
        level = level * one(*cut)
    return level


def bell_draw(key, shape, deviation, reach, cuts=(), held_as=jnp.bfloat16):
    result = jax.random.normal(key, shape, jnp.float32) * deviation
    if len(cuts) > 0:
        result = level_of(key, shape, cuts, -0.22, 0.18) * result
    return jnp.clip(result, min=-reach, max=reach).astype(held_as)


def gaussian_with(key, shape, deviation, limit, cuts, heavy, held_as=jnp.bfloat16):
    values = deviation * jax.random.normal(key, shape, jnp.float32)
    if cuts:
        values = values * level_of(key, shape, cuts, -0.22, 0.18)
    return jnp.clip(strengthened(values, jax.random.fold_in(key, 3), *heavy), -limit, limit).astype(held_as)


def setup_inputs(seed: int = 0) -> dict:
    seeds = jax.random.split(jax.random.key(seed), 19)
    pixels = bell_draw(seeds[0], (N_ROW * TILE_R, N_COL * TILE_C, PD), 1.0, 6.0, ((0, 4), (1, 8)))
    text = bell_draw(seeds[1], (ROWS * 3 * TEXT, D), 1.0, 6.0, ((0, 32),))
    token_source = draw_token_source(jax.random.fold_in(seeds[18], 71), 0)
    example_ids = draw_example_ids(jax.random.fold_in(seeds[18], 71), 0)
    cotangent = gaussian_with(seeds[4], (TOKENS, D), 1.0, 6.0, ((0, 32),), (0, 1, 32, 2.75))
    conv_weight = bell_draw(seeds[5], (PD, VW), PD ** -0.5, 0.25, ((1, 32),))
    conv_bias = bell_draw(seeds[6], (VW,), 0.5, 3.0, ((0, 32),))
    proj_weight = bell_draw(seeds[7], (VW, D), VW ** -0.5, 0.15625, ((1, 32),))
    proj_bias = bell_draw(seeds[8], (D,), 0.5, 3.0, ((0, 32),))
    first_gain = jnp.clip(1.0 + 0.18 * jax.random.normal(seeds[9], (D,), jnp.float32), 0.099609375, 1.8984375).astype(jnp.bfloat16)
    query_weight = bell_draw(seeds[10], (D, D), D ** -0.5, 0.1875, ((0, 32),))
    key_weight = bell_draw(seeds[11], (D, D), D ** -0.5, 0.1875, ((0, 32),))
    value_weight = bell_draw(seeds[12], (D, D), D ** -0.5, 0.1875, ((0, 32),))
    out_weight = bell_draw(seeds[13], (D, D), (max(D // 256, 1)) ** -0.5, 3.0, ((1, 32),))
    second_gain = jnp.clip(1.0 + 0.18 * jax.random.normal(seeds[14], (D,), jnp.float32), 0.099609375, 1.8984375).astype(jnp.bfloat16)
    gate_weight = bell_draw(seeds[15], (D, FF), D ** -0.5, 0.1875, ((0, 32),))
    up_weight = bell_draw(seeds[16], (D, FF), D ** -0.5, 0.1875, ((0, 32),))
    down_weight = bell_draw(seeds[17], (FF, D), FF ** -0.5, 0.109375, ((1, 32),))
    return dict(pixels=pixels, text=text, token_source=token_source, example_ids=example_ids, cotangent=cotangent, conv_weight=conv_weight, conv_bias=conv_bias, proj_weight=proj_weight, proj_bias=proj_bias, first_gain=first_gain, query_weight=query_weight, key_weight=key_weight, value_weight=value_weight, out_weight=out_weight, second_gain=second_gain, gate_weight=gate_weight, up_weight=up_weight, down_weight=down_weight)


@jax.custom_vjp
def low(v):
    return lax.optimization_barrier(v.astype(jnp.bfloat16)).astype(jnp.float32)

@jax.custom_vjp
def low_back(v):
    return v

def low_keep(v):
    return (low(v), None)

def low_pass(kept, grad):
    return (grad,)

def back_keep(v):
    return (v, None)

def back_low(kept, grad):
    return (low(grad),)
low.defvjp(low_keep, low_pass)
low_back.defvjp(back_keep, back_low)

def product(left, right):
    return jnp.dot(left, right, precision=lax.Precision.HIGHEST)

def normed(values, gain):
    return values * lax.rsqrt(lax.optimization_barrier(jnp.mean(values * values, axis=-1, keepdims=True)) + 1e-06) * gain

def gelu_tanh(values):
    return jax.nn.gelu(values, approximate=True)

def head_attention(query, keys, values, same_example):
    scores = low_back(jnp.where(same_example, product(query, keys.T) * 0.125, -1000000000.0))
    chances = low(jax.nn.softmax(scores, axis=-1))
    return product(chances, values)

def split_heads(values):
    return values.reshape(ROW, H, HD).transpose(1, 0, 2)

def block_row(tokens, example_row, query_mat, key_mat, value_mat, out_mat, gain_one, gain_two, gate_mat, up_mat, down_mat):
    same_example = example_row[:, None] == example_row[None, :]
    normal_one = low(normed(tokens, gain_one))
    queries = low(low_back(product(normal_one, query_mat)))
    keys_all = low(low_back(product(normal_one, key_mat)))
    values_all = low(low_back(product(normal_one, value_mat)))
    attended = lax.map(lambda parts: jax.checkpoint(head_attention)(parts[0], parts[1], parts[2], same_example), (split_heads(queries), split_heads(keys_all), split_heads(values_all)))
    mixed = low(low_back(attended.transpose(1, 0, 2).reshape(ROW, D)))
    middle = tokens + low_back(product(mixed, out_mat))
    normal_two = low(normed(middle, gain_two))
    gate = low_back(product(normal_two, gate_mat))
    upward = low_back(product(normal_two, up_mat))
    hidden = low(gelu_tanh(gate) * upward)
    return middle + product(hidden, down_mat)

def reference(pixels, text, token_source, example_ids, cotangent, conv_weight, conv_bias, proj_weight, proj_bias, first_gain, query_weight, key_weight, value_weight, out_weight, second_gain, gate_weight, up_weight, down_weight):
    text_rows = text.astype(jnp.float32).reshape(ROWS, 3 * TEXT, D)
    sources = token_source.reshape(ROWS, ROW)
    example_rows = example_ids.reshape(ROWS, ROW)

    def forward(pixel_values, conv_mat, conv_add, proj_mat, proj_add, gain_one, query_mat, key_mat, value_mat, out_mat, gain_two, gate_mat, up_mat, down_mat):
        patch_rows = pixel_values.reshape(-1, PD)
        visual = low(low_back(product(patch_rows, conv_mat) + conv_add))
        embedded = low(low_back(product(visual, proj_mat) + proj_add))
        tiles = embedded.reshape(N_ROW, TILE_R, N_COL, TILE_C, D).transpose(0, 2, 1, 3, 4)
        tiles = tiles.reshape(N_ROW * N_COL, N_ROW * N_COL, -1, D).transpose(1, 0, 2, 3)
        slots = tiles.reshape(ROWS, PATCH_SLOTS, D)
        pooled = jnp.concatenate((slots, text_rows), axis=1)
        tokens = jax.vmap(lambda pooled_row, chosen: pooled_row[chosen])(pooled, sources)

        def step(carry, parts):
            return (carry, jax.checkpoint(block_row)(parts[0], parts[1], query_mat, key_mat, value_mat, out_mat, gain_one, gain_two, gate_mat, up_mat, down_mat))
        _, outputs = lax.scan(step, jnp.zeros((), jnp.float32), (tokens, example_rows))
        return outputs.reshape(TOKENS, D)
    inputs = tuple((arr.astype(jnp.float32) for arr in (pixels, conv_weight, conv_bias, proj_weight, proj_bias, first_gain, query_weight, key_weight, value_weight, out_weight, second_gain, gate_weight, up_weight, down_weight)))
    output, pull = jax.vjp(forward, *inputs)
    grads = pull(cotangent.astype(jnp.float32))
    return (output.astype(jnp.bfloat16), grads[0], grads[1], grads[2], grads[3], grads[4], grads[5], grads[6], grads[7], grads[8], grads[9], grads[10], grads[11], grads[12], grads[13])
```

```python
import jax
import jax.numpy as jnp
from jax import lax
from jax.sharding import PartitionSpec as P

D = 1024
H = 16
HD = 64
PATCH_SLOTS = 1024
ROW = 1152
LANE = 128
F32 = jnp.float32
BF16 = jnp.bfloat16


def gelu_tanh(values):
    return jax.nn.gelu(values, approximate=True)


def matmul(left, right):
    return jnp.dot(left, right, preferred_element_type=F32)


def left_contract(left, right):
    return lax.dot_general(left, right, (((0,), (0,)), ((), ())), preferred_element_type=F32)


def right_contract(left, right):
    return lax.dot_general(left, right, (((1,), (1,)), ((), ())), preferred_element_type=F32)


def split_heads(values):
    return values.reshape(values.shape[0], H, HD).transpose(1, 0, 2)


def merge_heads(values):
    return values.transpose(1, 0, 2).reshape(values.shape[1], H * HD)


def masked_scores(query, keys, same_example):
    return jnp.where(same_example, right_contract(query, keys) * 0.125, -1000000000.0)


def attend(queries, keys_all, values_all, examples):
    same_example = examples[:, None] == examples[None, :]

    def one_head(pieces):
        query, keys, values = pieces
        scores = masked_scores(query, keys, same_example)
        row_max = jnp.max(scores, axis=-1, keepdims=True)
        powers = jnp.exp(scores - row_max)
        totals = jnp.sum(powers, axis=-1, keepdims=True)
        chances = (powers / totals).astype(BF16)
        return (matmul(chances, values).astype(BF16), (row_max + jnp.log(totals))[:, 0])

    outputs, logsum = lax.map(
        one_head, (split_heads(queries), split_heads(keys_all), split_heads(values_all))
    )
    return (merge_heads(outputs), logsum)


def attend_back(queries, keys_all, values_all, grads_all, logsum, examples):
    same_example = examples[:, None] == examples[None, :]

    def one_head(pieces):
        query, keys, values, grads, logs = pieces
        scores = masked_scores(query, keys, same_example)
        chances = jnp.exp(scores - logs[:, None])
        grad_chances = right_contract(grads, values)
        deltas = jnp.sum(chances * grad_chances, axis=-1, keepdims=True)
        grad_scores = (chances * (grad_chances - deltas)).astype(BF16)
        return (
            (matmul(grad_scores, keys) * 0.125).astype(BF16),
            (left_contract(grad_scores, query) * 0.125).astype(BF16),
            left_contract(chances.astype(BF16), grads).astype(BF16),
        )

    grads = lax.map(
        one_head,
        (
            split_heads(queries),
            split_heads(keys_all),
            split_heads(values_all),
            split_heads(grads_all),
            logsum,
        ),
    )
    return jnp.concatenate([merge_heads(part) for part in grads], axis=1)


def pad_to(values, rows, columns):
    return jnp.pad(values, ((0, rows - values.shape[0]), (0, columns - values.shape[1])))


def lanes_up(size):
    return -(-size // LANE) * LANE


class Halver:
    def __init__(self, mesh):
        self.sizes = {name: mesh.shape[name] for name in ("row", "col")}
        bits = {name: size.bit_length() - 1 for name, size in self.sizes.items()}
        self.places = [("row", b) for b in reversed(range(bits["row"]))]
        self.places += [("col", b) for b in reversed(range(bits["col"]))]
        rows = [("row", b) for b in range(bits["row"])]
        cols = [("col", b) for b in range(bits["col"])]
        self.first = rows[0]
        self.orders = (rows[1:] + cols, cols[:1] + rows[1:] + cols[1:])

    def stage(self, values, live, place, last):
        axis, bit = place
        at = live.index(place)
        pre = 2**at
        post = values.shape[0] // (2 * pre)
        parts = values.reshape(pre, 2, post, values.shape[1])
        mine = (lax.axis_index(axis) >> bit) & 1
        send = lax.dynamic_index_in_dim(parts, 1 - mine, 1, keepdims=False)
        keep = lax.dynamic_index_in_dim(parts, mine, 1, keepdims=False)
        size = self.sizes[axis]
        got = lax.ppermute(send, axis, [(i, i ^ (1 << bit)) for i in range(size)])
        total = (keep.astype(F32) + got.astype(F32)).reshape(pre * post, values.shape[1])
        live = [other for other in live if other != place]
        return (total if last else total.astype(BF16)), live

    def chain(self, values, live, order):
        for k, place in enumerate(order):
            values, live = self.stage(values, live, place, k == len(order) - 1)
        return values

    def scatter(self, values, cut=True):
        values, live = self.stage(values.astype(BF16), self.places, self.first, False)
        width = values.shape[1]
        if not cut:
            return self.chain(values, live, self.orders[0])
        half = lanes_up(width // 2)
        parts = (values[:, :half], values[:, half:])
        done = [self.chain(part, live, order) for part, order in zip(parts, self.orders)]
        return jnp.concatenate(done, axis=1)


def solution(mesh):
    both = ("row", "col")
    devices = mesh.shape["row"] * mesh.shape["col"]
    halver = Halver(mesh)

    def shards(
        pixels,
        text,
        token_source,
        example_ids,
        cotangent,
        conv_weight,
        conv_bias,
        proj_weight,
        proj_bias,
        first_gain,
        query_weight,
        key_weight,
        value_weight,
        out_weight,
        second_gain,
        gate_weight,
        up_weight,
        down_weight,
    ):
        pixel_depth = pixels.shape[-1]
        vision, block = proj_weight.shape
        vision_block = conv_weight.shape[1]
        hidden_width = gate_weight.shape[1]
        pixel_lanes = lanes_up(pixel_depth + 1)

        folds = -(-vision_block // block)
        conv_local = jnp.concatenate((conv_weight.T, conv_bias[:, None]), axis=1)
        conv_local = pad_to(conv_local, folds * block, pixel_lanes)
        vectors = jnp.stack((proj_bias, first_gain, second_gain), axis=1)
        pieces = [conv_local[f * block : (f + 1) * block] for f in range(folds)]
        pieces += [proj_weight.T, pad_to(vectors, block, LANE)]
        pieces += [query_weight, key_weight, value_weight, out_weight.T]
        front = lax.all_gather(jnp.concatenate(pieces, axis=1), both, axis=0, tiled=True)
        ffn = lax.all_gather(
            jnp.concatenate((gate_weight, up_weight, down_weight.T), axis=1),
            both,
            axis=0,
            tiled=True,
        )
        at = folds * pixel_lanes
        conv_t = front[:, :at].reshape(devices, block, folds, pixel_lanes).transpose(0, 2, 1, 3)
        conv_t = conv_t.reshape(devices, folds * block, pixel_lanes)[:, :vision_block]
        conv_t = conv_t.reshape(devices * vision_block, pixel_lanes)
        proj_t = front[:, at : at + vision]
        at += vision
        vector_rows = front[:, at : at + LANE].T.astype(F32)
        proj_add, gain_first, gain_second = vector_rows[0], vector_rows[1], vector_rows[2]
        at += LANE
        qkv_whole = front[:, at : at + 3 * D]
        out_t = front[:, at + 3 * D :]
        gate_whole = ffn[:, :hidden_width]
        up_whole = ffn[:, hidden_width : 2 * hidden_width]
        down_t = ffn[:, 2 * hidden_width :]

        cells = pixels.reshape(-1, pixel_depth)
        ones = jnp.ones((cells.shape[0], 1), BF16)
        cells = pad_to(jnp.concatenate((cells, ones), axis=1), cells.shape[0], pixel_lanes)
        slots = lax.all_to_all(cells, both, split_axis=0, concat_axis=0, tiled=True)
        source = token_source[:, None]
        is_patch = source < PATCH_SLOTS
        pick_patch = (source == lax.iota(jnp.int32, PATCH_SLOTS)[None, :]).astype(BF16)
        text_ids = lax.iota(jnp.int32, text.shape[0]) + PATCH_SLOTS
        pick_text = (source == text_ids[None, :]).astype(BF16)
        patches = matmul(pick_patch, slots).astype(BF16)
        text_tokens = matmul(pick_text, text).astype(BF16)

        visual = right_contract(patches, conv_t).astype(BF16)
        embedded = (right_contract(visual, proj_t) + proj_add).astype(BF16)
        residual = jnp.where(is_patch, embedded, text_tokens).astype(F32)
        scale_one = lax.rsqrt(jnp.mean(residual * residual, axis=-1, keepdims=True) + 1e-06)
        normal_in = (residual * scale_one * gain_first).astype(BF16)
        qkv = matmul(normal_in, qkv_whole).astype(BF16)
        queries, keys_all, values_all = qkv[:, :D], qkv[:, D : 2 * D], qkv[:, 2 * D :]
        mixed, logsum = attend(queries, keys_all, values_all, example_ids)
        middle = residual + right_contract(mixed, out_t)
        scale_two = lax.rsqrt(jnp.mean(middle * middle, axis=-1, keepdims=True) + 1e-06)
        normal_mid = (middle * scale_two * gain_second).astype(BF16)
        gate = matmul(normal_mid, gate_whole)
        upward = matmul(normal_mid, up_whole)
        gate_act, gelu_pull = jax.vjp(gelu_tanh, gate)
        hidden = (gate_act * upward).astype(BF16)
        output = (middle + right_contract(hidden, down_t)).astype(BF16)

        grad_hidden = matmul(cotangent, down_t)
        grad_gate = gelu_pull(grad_hidden * upward)[0].astype(BF16)
        grad_upward = (grad_hidden * gate_act).astype(BF16)
        grad_down_t = halver.scatter(left_contract(cotangent, hidden))
        grad_gate_w = halver.scatter(left_contract(normal_mid, grad_gate))
        grad_up_w = halver.scatter(left_contract(normal_mid, grad_upward))
        grad_mid = right_contract(grad_gate, gate_whole) + right_contract(grad_upward, up_whole)
        gain_two_sum = jnp.sum(grad_mid * middle * scale_two, axis=0)
        pulled = grad_mid * gain_second
        pulled_mean = jnp.mean(pulled * middle, axis=-1, keepdims=True)
        grad_middle = cotangent.astype(F32) + scale_two * (
            pulled - middle * (scale_two * scale_two) * pulled_mean
        )
        grad_branch = grad_middle.astype(BF16)

        grad_out_t = halver.scatter(left_contract(grad_branch, mixed))
        grad_mixed = matmul(grad_branch, out_t).astype(BF16)
        grad_qkv = attend_back(queries, keys_all, values_all, grad_mixed, logsum, example_ids)
        grad_qkv_w = halver.scatter(left_contract(normal_in, grad_qkv))
        grad_normal = right_contract(grad_qkv, qkv_whole)
        gain_one_sum = jnp.sum(grad_normal * residual * scale_one, axis=0)
        pulled = grad_normal * gain_first
        pulled_mean = jnp.mean(pulled * residual, axis=-1, keepdims=True)
        grad_residual = grad_middle + scale_one * (
            pulled - residual * (scale_one * scale_one) * pulled_mean
        )

        grad_embedded = jnp.where(is_patch, grad_residual, 0.0).astype(BF16)
        grad_visual = matmul(grad_embedded, proj_t).astype(BF16)
        grad_patches = matmul(grad_visual, conv_t).astype(BF16)
        grad_slots = left_contract(pick_patch, grad_patches).astype(BF16)
        grad_cells = lax.all_to_all(grad_slots, both, split_axis=0, concat_axis=0, tiled=True)
        grad_pixels = grad_cells[:, :pixel_depth].astype(F32).reshape(pixels.shape)
        grad_proj_t = halver.scatter(left_contract(grad_embedded, visual))
        grad_conv_t = halver.scatter(left_contract(grad_visual, patches))
        proj_add_sum = jnp.sum(grad_embedded.astype(F32), axis=0)
        sums = jnp.stack((proj_add_sum, gain_one_sum, gain_two_sum), axis=0)
        sums = halver.scatter(pad_to(sums, LANE, D).T, cut=False)
        return (
            output,
            grad_pixels,
            grad_conv_t[:, :pixel_depth].T,
            grad_conv_t[:, pixel_depth],
            grad_proj_t.T,
            sums[:, 0],
            sums[:, 1],
            grad_qkv_w[:, :D],
            grad_qkv_w[:, D : 2 * D],
            grad_qkv_w[:, 2 * D :],
            grad_out_t.T,
            sums[:, 2],
            grad_gate_w,
            grad_up_w,
            grad_down_t.T,
        )

    rows = P(both, None)
    columns = P(None, both)
    vector = P(both)
    tiles = P("row", "col", None)
    return jax.shard_map(
        shards,
        mesh=mesh,
        in_specs=(
            tiles,
            rows,
            vector,
            vector,
            rows,
            columns,
            vector,
            columns,
            vector,
            vector,
            rows,
            rows,
            rows,
            columns,
            vector,
            rows,
            rows,
            columns,
        ),
        out_specs=(
            rows,
            tiles,
            columns,
            vector,
            columns,
            vector,
            vector,
            rows,
            rows,
            rows,
            columns,
            vector,
            rows,
            rows,
            columns,
        ),
        check_vma=False,
    )
```

```python
import jax
import jax.numpy as jnp
from jax import lax
from jax.experimental import pallas as pl
from jax.experimental.pallas import tpu as pltpu
from jax.sharding import PartitionSpec as P

D = 1024
H = 16
HD = 64
PATCH_SLOTS = 1024
ROW = 1152
SPAN = 384
LANE = 128
PAIRS = D // LANE
F32 = jnp.float32
BF16 = jnp.bfloat16


def gelu_tanh(values):
    return jax.nn.gelu(values, approximate=True)


def matmul(left, right):
    return jnp.dot(left, right, preferred_element_type=F32)


def left_contract(left, right):
    return lax.dot_general(left, right, (((0,), (0,)), ((), ())), preferred_element_type=F32)


def right_contract(left, right):
    return lax.dot_general(left, right, (((1,), (1,)), ((), ())), preferred_element_type=F32)


def low_lanes(rows):
    return lax.broadcasted_iota(jnp.int32, (rows, LANE), 1) < HD


def attend_kernel(ids_ref, q_ref, k_ref, v_ref, o_ref, l_ref):
    single = ids_ref[0] == ids_ref[ROW - 1]

    def tile(t, base, keys):
        at = pl.ds(pl.multiple_of(t * SPAN, SPAN), SPAN)
        query = q_ref[at, :] * 0.125
        key = k_ref[pl.ds(base, keys), :]
        value = v_ref[pl.ds(base, keys), :]
        low, low_keys = low_lanes(SPAN), low_lanes(keys)
        mixes, tops = [], []
        for h in range(2):
            mine = low if h == 0 else ~low
            mine_keys = low_keys if h == 0 else ~low_keys
            scores = right_contract(jnp.where(mine, query, jnp.zeros_like(query)), key)
            top = jnp.max(scores, axis=-1, keepdims=True)
            powers = jnp.exp(scores - top).astype(BF16)
            mixes.append(matmul(powers, jnp.where(mine_keys, value, jnp.ones_like(value))))
            tops.append(top)
        total = pltpu.roll(jnp.where(low, mixes[1], mixes[0]), HD, 1)
        o_ref[at, :] = (jnp.where(low, mixes[0], mixes[1]) / total).astype(BF16)
        logs = (jnp.where(low, tops[0], tops[1]) + jnp.log(total)).T
        l_ref[0, :, at] = jnp.concatenate([logs[0:8], logs[HD : HD + 8]], axis=0)

    @pl.when(single)
    def _():
        lax.fori_loop(0, ROW // SPAN, lambda t, c: (tile(t, 0, ROW), c)[1], 0)

    @pl.when(jnp.logical_not(single))
    def _():
        def body(t, c):
            tile(t, pl.multiple_of(t * SPAN, SPAN), SPAN)
            return c

        lax.fori_loop(0, ROW // SPAN, body, 0)


def attend(qkv, ids):
    def columns(offset):
        return pl.BlockSpec((ROW, LANE), lambda i, ids: (0, offset + i))

    return pl.pallas_call(
        attend_kernel,
        out_shape=(
            jax.ShapeDtypeStruct((ROW, D), BF16),
            jax.ShapeDtypeStruct((PAIRS, 16, ROW), F32),
        ),
        grid_spec=pltpu.PrefetchScalarGridSpec(
            num_scalar_prefetch=1,
            grid=(PAIRS,),
            in_specs=[columns(0), columns(PAIRS), columns(2 * PAIRS)],
            out_specs=[columns(0), pl.BlockSpec((1, 16, ROW), lambda i, ids: (i, 0, 0))],
        ),
        compiler_params=pltpu.CompilerParams(vmem_limit_bytes=40 << 20),
        cost_estimate=pl.CostEstimate(
            flops=16 * ROW * ROW * D, bytes_accessed=8 * ROW * D, transcendentals=H * ROW * ROW
        ),
    )(ids, qkv, qkv, qkv)


def back_kernel(ids_ref, q_ref, k_ref, v_ref, g_ref, o_ref, l_ref, *rest):
    dq_ref, dk_ref, dv_ref, key_sum, value_sum = rest[-5:]
    single = ids_ref[0] == ids_ref[ROW - 1]

    def tile(t, base, keys, first):
        at = pl.ds(pl.multiple_of(t * SPAN, SPAN), SPAN)
        from_keys = pl.ds(base, keys)
        query, grad = q_ref[at, :] * 0.125, g_ref[at, :]
        key, value = k_ref[from_keys, :], v_ref[from_keys, :]
        low = low_lanes(SPAN)
        blank = jnp.zeros_like(query)
        products = grad.astype(F32) * o_ref[at, :].astype(F32)
        row_head = lax.broadcasted_iota(jnp.int32, (16, LANE), 0) // 8
        lane_head = lax.broadcasted_iota(jnp.int32, (16, LANE), 1) // HD
        delta = lax.dot_general(
            (row_head == lane_head).astype(F32),
            products,
            (((1,), (1,)), ((), ())),
            preferred_element_type=F32,
            precision=lax.Precision.HIGHEST,
        )
        key_t = key.T
        grad_query, grad_key, grad_value = [], 0.0, 0.0
        for h in range(2):
            mine = low if h == 0 else ~low
            query_h, grad_h = jnp.where(mine, query, blank), jnp.where(mine, grad, blank)
            chances = jnp.exp(right_contract(key, query_h) - l_ref[0, 8 * h : 8 * h + 1, at])
            grad_chances = right_contract(value, grad_h)
            grad_scores = (chances * (grad_chances - delta[8 * h : 8 * h + 1, :])).astype(BF16)
            grad_query.append(matmul(key_t[h * HD : (h + 1) * HD, :], grad_scores))
            grad_value += matmul(chances.astype(BF16), grad_h)
            grad_key += matmul(grad_scores, query_h)
        dq_ref[at, :] = (jnp.concatenate(grad_query, axis=0) * 0.125).T.astype(BF16)
        if first is None:
            dk_ref[from_keys, :] = grad_key.astype(BF16)
            dv_ref[from_keys, :] = grad_value.astype(BF16)
            return

        @pl.when(first)
        def _():
            key_sum[...] = grad_key
            value_sum[...] = grad_value

        @pl.when(jnp.logical_not(first))
        def _():
            key_sum[...] += grad_key
            value_sum[...] += grad_value

    @pl.when(single)
    def _():
        lax.fori_loop(0, ROW // SPAN, lambda t, c: (tile(t, 0, ROW, t == 0), c)[1], 0)
        dk_ref[...] = key_sum[...].astype(BF16)
        dv_ref[...] = value_sum[...].astype(BF16)

    @pl.when(jnp.logical_not(single))
    def _():
        def body(t, c):
            tile(t, pl.multiple_of(t * SPAN, SPAN), SPAN, None)
            return c

        lax.fori_loop(0, ROW // SPAN, body, 0)


def attend_back(qkv, grads, mixed, logsum, ids, start, count, held):
    def columns(offset):
        return pl.BlockSpec((ROW, LANE), lambda i, ids: (0, offset + start + i))

    logs = pl.BlockSpec((1, 16, ROW), lambda i, ids: (start + i, 0, 0))
    anywhere = [pl.BlockSpec(memory_space=pl.ANY)] * len(held)
    whole = jax.ShapeDtypeStruct((ROW, D), BF16)
    inputs = [columns(0), columns(PAIRS), columns(2 * PAIRS), columns(0), columns(0), logs]
    return pl.pallas_call(
        back_kernel,
        out_shape=(whole, whole, whole),
        grid_spec=pltpu.PrefetchScalarGridSpec(
            num_scalar_prefetch=1,
            grid=(count,),
            in_specs=inputs + anywhere,
            out_specs=[columns(0)] * 3,
            scratch_shapes=[pltpu.VMEM((ROW, LANE), F32)] * 2,
        ),
        input_output_aliases={7 + k: k for k in range(len(held))},
        compiler_params=pltpu.CompilerParams(vmem_limit_bytes=40 << 20),
        cost_estimate=pl.CostEstimate(
            flops=40 * ROW * ROW * LANE * count,
            bytes_accessed=16 * ROW * LANE * count,
            transcendentals=2 * count * ROW * ROW,
        ),
    )(ids, qkv, qkv, qkv, grads, mixed, logsum, *held)


def pad_to(values, rows, columns):
    return jnp.pad(values, ((0, rows - values.shape[0]), (0, columns - values.shape[1])))


def lanes_up(size):
    return -(-size // LANE) * LANE


class Places:
    def __init__(self, mesh):
        self.sizes = {name: mesh.shape[name] for name in ("row", "col")}
        bits = {name: size.bit_length() - 1 for name, size in self.sizes.items()}
        self.live = [("row", b) for b in reversed(range(bits["row"]))]
        self.live += [("col", b) for b in reversed(range(bits["col"]))]
        rows = [("row", b) for b in range(bits["row"])]
        cols = [("col", b) for b in range(bits["col"])]
        self.first = rows[0]
        self.orders = (rows[1:] + cols, cols[:1] + rows[1:] + cols[1:])

    def mine(self, place):
        return (lax.axis_index(place[0]) >> place[1]) & 1

    def swap(self, values, place):
        axis, bit = place
        pairs = [(i, i ^ (1 << bit)) for i in range(self.sizes[axis])]
        return lax.ppermute(values, axis, pairs)

    def split(self, values, live, place, dim=0):
        pre = 2 ** live.index(place)
        shape = values.shape
        parts = values.reshape(shape[:dim] + (pre, 2, -1) + shape[dim + 1 :])
        half = shape[:dim] + (shape[dim] // 2,) + shape[dim + 1 :]
        mine = self.mine(place)
        send = lax.dynamic_index_in_dim(parts, 1 - mine, dim + 1, keepdims=False)
        keep = lax.dynamic_index_in_dim(parts, mine, dim + 1, keepdims=False)
        return send.reshape(half), keep.reshape(half)


def added(keep, got):
    return keep.astype(F32) + got.astype(F32)


class Chain:
    def __init__(self, places, values, order):
        self.places = places
        self.values = values
        self.live = [place for place in places.live if place != places.first]
        self.order = places.orders[order]
        self.at = 0

    def prepare(self):
        place = self.order[self.at]
        send, self.keep = self.places.split(self.values.astype(BF16), self.live, place)
        return send

    def launch(self, send):
        place = self.order[self.at]
        self.values = added(self.keep, self.places.swap(send, place))
        self.live = [other for other in self.live if other != place]
        self.at += 1

    def finish(self):
        while self.at < len(self.order):
            self.launch(self.prepare())
        return self.values


def tick(chains, *values):
    sends = tuple(chain.prepare() for chain in chains)
    held = lax.optimization_barrier((sends, values))
    for chain, send in zip(chains, held[0]):
        chain.launch(send)
    return held[1]


def halves(places, values):
    cut = lanes_up(values.shape[1] // 2)
    return [Chain(places, values[:, :cut], 0), Chain(places, values[:, cut:], 1)]


def joined(chains):
    return jnp.concatenate([chain.finish() for chain in chains], axis=1)


def solution(mesh):
    both = ("row", "col")
    devices = mesh.shape["row"] * mesh.shape["col"]
    places = Places(mesh)

    def shards(
        pixels,
        text,
        token_source,
        example_ids,
        cotangent,
        conv_weight,
        conv_bias,
        proj_weight,
        proj_bias,
        first_gain,
        query_weight,
        key_weight,
        value_weight,
        out_weight,
        second_gain,
        gate_weight,
        up_weight,
        down_weight,
    ):
        pixel_depth = pixels.shape[-1]
        vision, block = proj_weight.shape
        vision_block = conv_weight.shape[1]
        hidden_width = gate_weight.shape[1]
        pixel_lanes = lanes_up(pixel_depth + 1)

        folds = -(-vision_block // block)
        conv_local = jnp.concatenate((conv_weight.T, conv_bias[:, None]), axis=1)
        conv_local = pad_to(conv_local, folds * block, pixel_lanes)
        vectors = jnp.stack((proj_bias, first_gain, second_gain), axis=1)
        pieces = [conv_local[f * block : (f + 1) * block] for f in range(folds)]
        pieces += [proj_weight.T, pad_to(vectors, block, LANE)]
        pieces += [query_weight, key_weight, value_weight, out_weight.T]
        front = lax.all_gather(jnp.concatenate(pieces, axis=1), both, axis=0, tiled=True)
        ffn = lax.all_gather(
            jnp.concatenate((gate_weight, up_weight, down_weight.T), axis=1),
            both,
            axis=0,
            tiled=True,
        )
        at = folds * pixel_lanes
        conv_t = front[:, :at].reshape(devices, block, folds, pixel_lanes).transpose(0, 2, 1, 3)
        conv_t = conv_t.reshape(devices, folds * block, pixel_lanes)[:, :vision_block]
        conv_t = conv_t.reshape(devices * vision_block, pixel_lanes)
        proj_t = front[:, at : at + vision]
        at += vision
        vector_rows = front[:, at : at + LANE].T.astype(F32)
        proj_add, gain_first, gain_second = vector_rows[0], vector_rows[1], vector_rows[2]
        at += LANE
        qkv_whole = front[:, at : at + 3 * D]
        out_t = front[:, at + 3 * D :]
        gate_whole = ffn[:, :hidden_width]
        up_whole = ffn[:, hidden_width : 2 * hidden_width]
        down_t = ffn[:, 2 * hidden_width :]

        cells = pixels.reshape(-1, pixel_depth)
        ones = jnp.ones((cells.shape[0], 1), BF16)
        cells = pad_to(jnp.concatenate((cells, ones), axis=1), cells.shape[0], pixel_lanes)
        slots = lax.all_to_all(cells, both, split_axis=0, concat_axis=0, tiled=True)
        source = token_source[:, None]
        is_patch = source < PATCH_SLOTS
        pick_patch = (source == lax.iota(jnp.int32, PATCH_SLOTS)[None, :]).astype(BF16)
        text_ids = lax.iota(jnp.int32, text.shape[0]) + PATCH_SLOTS
        pick_text = (source == text_ids[None, :]).astype(BF16)
        patches = matmul(pick_patch, slots).astype(BF16)
        text_tokens = matmul(pick_text, text).astype(BF16)

        visual = right_contract(patches, conv_t).astype(BF16)
        embedded = (right_contract(visual, proj_t) + proj_add).astype(BF16)
        residual = jnp.where(is_patch, embedded, text_tokens).astype(F32)
        scale_one = lax.rsqrt(jnp.mean(residual * residual, axis=-1, keepdims=True) + 1e-06)
        normal_in = (residual * scale_one * gain_first).astype(BF16)
        qkv = matmul(normal_in, qkv_whole).astype(BF16)
        mixed, logsum = attend(qkv, example_ids)
        middle = residual + right_contract(mixed, out_t)
        scale_two = lax.rsqrt(jnp.mean(middle * middle, axis=-1, keepdims=True) + 1e-06)
        normal_mid = (middle * scale_two * gain_second).astype(BF16)
        gate = matmul(normal_mid, gate_whole)
        upward = matmul(normal_mid, up_whole)
        gate_act, gelu_pull = jax.vjp(gelu_tanh, gate)
        hidden = (gate_act * upward).astype(BF16)
        output = (middle + right_contract(hidden, down_t)).astype(BF16)

        def shares(left):
            return places.split(left, places.live, places.first, dim=1)

        def partial(left, right):
            return left_contract(left, right).astype(BF16)

        theirs, ours = shares(cotangent)
        down_send, grad_out = lax.optimization_barrier((partial(theirs, hidden), cotangent))
        down_got = places.swap(down_send, places.first)
        grad_hidden = matmul(grad_out, down_t)
        grad_gate = gelu_pull(grad_hidden * upward)[0].astype(BF16)
        grad_upward = (grad_hidden * gate_act).astype(BF16)
        down = halves(places, added(partial(ours, hidden), down_got))
        theirs, ours = shares(normal_mid)
        gate_send, up_send = partial(theirs, grad_gate), partial(theirs, grad_upward)
        gate_send, up_send, grad_gate, grad_upward = tick(
            down, gate_send, up_send, grad_gate, grad_upward
        )
        gate_got = places.swap(gate_send, places.first)
        up_got = places.swap(up_send, places.first)
        grad_mid = right_contract(grad_gate, gate_whole) + right_contract(grad_upward, up_whole)
        gain_two_sum = jnp.sum(grad_mid * middle * scale_two, axis=0)
        pulled = grad_mid * gain_second
        pulled_mean = jnp.mean(pulled * middle, axis=-1, keepdims=True)
        grad_middle = cotangent.astype(F32) + scale_two * (
            pulled - middle * (scale_two * scale_two) * pulled_mean
        )
        grad_branch = grad_middle.astype(BF16)
        wide = [
            Chain(places, added(partial(ours, grad_gate), gate_got), 0),
            Chain(places, added(partial(ours, grad_upward), up_got), 1),
        ]

        (grad_branch,) = tick(wide + down, grad_branch)
        theirs, ours = shares(grad_branch)
        grad_mixed = matmul(grad_branch, out_t).astype(BF16)
        out_send, grad_mixed = lax.optimization_barrier((partial(theirs, mixed), grad_mixed))
        out_got = places.swap(out_send, places.first)
        step = PAIRS // 4

        def back(part, held):
            return attend_back(
                qkv, grad_mixed, mixed, logsum, example_ids, part * step, step, held
            )

        held = back(0, ())
        out = halves(places, added(partial(ours, mixed), out_got))
        grad_mixed, *held = tick(down + out, grad_mixed, *held)
        held = back(1, held)
        grad_mixed, *held = tick(wide + down + out, grad_mixed, *held)
        held = back(2, held)
        grad_mixed, *held = tick(wide + out, grad_mixed, *held)
        held = back(3, held)
        grad_qkv = tick(wide + out, *held)

        theirs, ours = shares(normal_in)
        sends, grad_qkv = lax.optimization_barrier(
            ([partial(theirs, part) for part in grad_qkv], grad_qkv)
        )
        gots = [places.swap(send, places.first) for send in sends]
        grad_normal = sum(
            right_contract(part, qkv_whole[:, k * D : (k + 1) * D])
            for k, part in enumerate(grad_qkv)
        )
        triple = [added(partial(ours, part), got) for part, got in zip(grad_qkv, gots)]
        attention = halves(places, jnp.concatenate(triple, axis=1))
        (grad_normal,) = tick(attention, grad_normal)
        gain_one_sum = jnp.sum(grad_normal * residual * scale_one, axis=0)
        pulled = grad_normal * gain_first
        pulled_mean = jnp.mean(pulled * residual, axis=-1, keepdims=True)
        grad_residual = grad_middle + scale_one * (
            pulled - residual * (scale_one * scale_one) * pulled_mean
        )

        grad_embedded = jnp.where(is_patch, grad_residual, 0.0).astype(BF16)
        grad_visual = matmul(grad_embedded, proj_t).astype(BF16)
        theirs, ours = shares(grad_embedded)
        proj_send = partial(theirs, visual)
        proj_send, grad_visual = tick(attention, proj_send, grad_visual)
        proj_got = places.swap(proj_send, places.first)
        grad_patches = matmul(grad_visual, conv_t).astype(BF16)
        grad_slots = left_contract(pick_patch, grad_patches).astype(BF16)
        conv_sum = partial(grad_visual, patches)
        conv_send, conv_keep = places.split(conv_sum, places.live, places.first)
        conv_send, grad_slots = lax.optimization_barrier((conv_send, grad_slots))
        conv_got = places.swap(conv_send, places.first)
        grad_cells = lax.all_to_all(grad_slots, both, split_axis=0, concat_axis=0, tiled=True)
        grad_pixels = grad_cells[:, :pixel_depth].astype(F32).reshape(pixels.shape)
        proj = halves(places, added(partial(ours, visual), proj_got))
        conv = halves(places, added(conv_keep, conv_got))
        proj_add_sum = jnp.sum(grad_embedded.astype(F32), axis=0)
        sums = jnp.stack((proj_add_sum, gain_one_sum, gain_two_sum), axis=0)
        sums_send, sums_keep = places.split(
            pad_to(sums, LANE, D).T.astype(BF16), places.live, places.first
        )
        sums = Chain(places, added(sums_keep, places.swap(sums_send, places.first)), 0).finish()
        grad_down_t, grad_out_t = joined(down), joined(out)
        grad_gate_w, grad_up_w = [chain.finish() for chain in wide]
        grad_qkv_w, grad_proj_t, grad_conv_t = joined(attention), joined(proj), joined(conv)
        return (
            output,
            grad_pixels,
            grad_conv_t[:, :pixel_depth].T,
            grad_conv_t[:, pixel_depth],
            grad_proj_t.T,
            sums[:, 0],
            sums[:, 1],
            grad_qkv_w[:, :D],
            grad_qkv_w[:, D : 2 * D],
            grad_qkv_w[:, 2 * D :],
            grad_out_t.T,
            sums[:, 2],
            grad_gate_w,
            grad_up_w,
            grad_down_t.T,
        )

    rows = P(both, None)
    columns = P(None, both)
    vector = P(both)
    tiles = P("row", "col", None)
    return jax.shard_map(
        shards,
        mesh=mesh,
        in_specs=(
            tiles,
            rows,
            vector,
            vector,
            rows,
            columns,
            vector,
            columns,
            vector,
            vector,
            rows,
            rows,
            rows,
            columns,
            vector,
            rows,
            rows,
            columns,
        ),
        out_specs=(
            rows,
            tiles,
            columns,
            vector,
            columns,
            vector,
            vector,
            rows,
            rows,
            rows,
            columns,
            vector,
            rows,
            rows,
            columns,
        ),
        check_vma=False,
    )
```

```python
import jax
import jax.numpy as jnp
from jax import lax
from jax.experimental import pallas as pl
from jax.experimental.pallas import tpu as pltpu
from jax.sharding import PartitionSpec as P

D = 1024
H = 16
HD = 64
PATCH_SLOTS = 1024
ROW = 1152
SPAN = 384
LANE = 128
PAIRS = D // LANE
F32 = jnp.float32
BF16 = jnp.bfloat16


def gelu_tanh(values):
    return jax.nn.gelu(values, approximate=True)


def matmul(left, right):
    return jnp.dot(left, right, preferred_element_type=F32)


def left_contract(left, right):
    return lax.dot_general(left, right, (((0,), (0,)), ((), ())), preferred_element_type=F32)


def right_contract(left, right):
    return lax.dot_general(left, right, (((1,), (1,)), ((), ())), preferred_element_type=F32)


def low_lanes(rows):
    return lax.broadcasted_iota(jnp.int32, (rows, LANE), 1) < HD


def attend_kernel(ids_ref, q_ref, k_ref, v_ref, o_ref, l_ref):
    single = ids_ref[0] == ids_ref[ROW - 1]

    def tile(t, base, keys):
        at = pl.ds(pl.multiple_of(t * SPAN, SPAN), SPAN)
        query = q_ref[at, :] * 0.125
        key = k_ref[pl.ds(base, keys), :]
        value = v_ref[pl.ds(base, keys), :]
        low, low_keys = low_lanes(SPAN), low_lanes(keys)
        mixes, tops = [], []
        for h in range(2):
            mine = low if h == 0 else ~low
            mine_keys = low_keys if h == 0 else ~low_keys
            scores = right_contract(jnp.where(mine, query, jnp.zeros_like(query)), key)
            top = jnp.max(scores, axis=-1, keepdims=True)
            powers = jnp.exp(scores - top).astype(BF16)
            mixes.append(matmul(powers, jnp.where(mine_keys, value, jnp.ones_like(value))))
            tops.append(top)
        total = pltpu.roll(jnp.where(low, mixes[1], mixes[0]), HD, 1)
        o_ref[at, :] = (jnp.where(low, mixes[0], mixes[1]) / total).astype(BF16)
        logs = (jnp.where(low, tops[0], tops[1]) + jnp.log(total)).T
        l_ref[0, :, at] = jnp.concatenate([logs[0:8], logs[HD : HD + 8]], axis=0)

    @pl.when(single)
    def _():
        lax.fori_loop(0, ROW // SPAN, lambda t, c: (tile(t, 0, ROW), c)[1], 0)

    @pl.when(jnp.logical_not(single))
    def _():
        def body(t, c):
            tile(t, pl.multiple_of(t * SPAN, SPAN), SPAN)
            return c

        lax.fori_loop(0, ROW // SPAN, body, 0)


def attend(qkv, ids):
    def part(which):
        return pl.BlockSpec((ROW, LANE), lambda i, ids: (0, 3 * i + which))

    return pl.pallas_call(
        attend_kernel,
        out_shape=(
            jax.ShapeDtypeStruct((ROW, D), BF16),
            jax.ShapeDtypeStruct((PAIRS, 16, ROW), F32),
        ),
        grid_spec=pltpu.PrefetchScalarGridSpec(
            num_scalar_prefetch=1,
            grid=(PAIRS,),
            in_specs=[part(0), part(1), part(2)],
            out_specs=[pl.BlockSpec((ROW, LANE), lambda i, ids: (0, i)), pl.BlockSpec((1, 16, ROW), lambda i, ids: (i, 0, 0))],
        ),
        compiler_params=pltpu.CompilerParams(vmem_limit_bytes=40 << 20),
        cost_estimate=pl.CostEstimate(
            flops=16 * ROW * ROW * D, bytes_accessed=8 * ROW * D, transcendentals=H * ROW * ROW
        ),
    )(ids, qkv, qkv, qkv)


def back_kernel(ids_ref, q_ref, k_ref, v_ref, g_ref, o_ref, l_ref, d_ref, key_sum, value_sum):
    single = ids_ref[0] == ids_ref[ROW - 1]

    def tile(t, base, keys, first):
        at = pl.ds(pl.multiple_of(t * SPAN, SPAN), SPAN)
        from_keys = pl.ds(base, keys)
        query, grad = q_ref[at, :] * 0.125, g_ref[at, :]
        key, value = k_ref[from_keys, :], v_ref[from_keys, :]
        low = low_lanes(SPAN)
        blank = jnp.zeros_like(query)
        products = grad.astype(F32) * o_ref[at, :].astype(F32)
        row_head = lax.broadcasted_iota(jnp.int32, (16, LANE), 0) // 8
        lane_head = lax.broadcasted_iota(jnp.int32, (16, LANE), 1) // HD
        delta = lax.dot_general(
            (row_head == lane_head).astype(F32),
            products,
            (((1,), (1,)), ((), ())),
            preferred_element_type=F32,
            precision=lax.Precision.HIGHEST,
        )
        key_t = key.T
        grad_query, grad_key, grad_value = [], 0.0, 0.0
        for h in range(2):
            mine = low if h == 0 else ~low
            query_h, grad_h = jnp.where(mine, query, blank), jnp.where(mine, grad, blank)
            chances = jnp.exp(right_contract(key, query_h) - l_ref[0, 8 * h : 8 * h + 1, at])
            grad_chances = right_contract(value, grad_h)
            grad_scores = (chances * (grad_chances - delta[8 * h : 8 * h + 1, :])).astype(BF16)
            grad_query.append(matmul(key_t[h * HD : (h + 1) * HD, :], grad_scores))
            grad_value += matmul(chances.astype(BF16), grad_h)
            grad_key += matmul(grad_scores, query_h)
        d_ref[at, :LANE] = (jnp.concatenate(grad_query, axis=0) * 0.125).T.astype(BF16)
        if first is None:
            d_ref[from_keys, LANE : 2 * LANE] = grad_key.astype(BF16)
            d_ref[from_keys, 2 * LANE :] = grad_value.astype(BF16)
            return

        @pl.when(first)
        def _():
            key_sum[...] = grad_key
            value_sum[...] = grad_value

        @pl.when(jnp.logical_not(first))
        def _():
            key_sum[...] += grad_key
            value_sum[...] += grad_value

    @pl.when(single)
    def _():
        lax.fori_loop(0, ROW // SPAN, lambda t, c: (tile(t, 0, ROW, t == 0), c)[1], 0)
        d_ref[:, LANE : 2 * LANE] = key_sum[...].astype(BF16)
        d_ref[:, 2 * LANE :] = value_sum[...].astype(BF16)

    @pl.when(jnp.logical_not(single))
    def _():
        def body(t, c):
            tile(t, pl.multiple_of(t * SPAN, SPAN), SPAN, None)
            return c

        lax.fori_loop(0, ROW // SPAN, body, 0)


def attend_back(qkv, grads, mixed, logsum, ids, start, count):
    def part(which):
        return pl.BlockSpec((ROW, LANE), lambda i, ids: (0, 3 * (start + i) + which))

    pair = pl.BlockSpec((ROW, LANE), lambda i, ids: (0, start + i))
    logs = pl.BlockSpec((1, 16, ROW), lambda i, ids: (start + i, 0, 0))
    return pl.pallas_call(
        back_kernel,
        out_shape=jax.ShapeDtypeStruct((ROW, 3 * LANE * count), BF16),
        grid_spec=pltpu.PrefetchScalarGridSpec(
            num_scalar_prefetch=1,
            grid=(count,),
            in_specs=[part(0), part(1), part(2), pair, pair, logs],
            out_specs=pl.BlockSpec((ROW, 3 * LANE), lambda i, ids: (0, i)),
            scratch_shapes=[pltpu.VMEM((ROW, LANE), F32)] * 2,
        ),
        compiler_params=pltpu.CompilerParams(vmem_limit_bytes=40 << 20),
        cost_estimate=pl.CostEstimate(
            flops=40 * ROW * ROW * LANE * count,
            bytes_accessed=16 * ROW * LANE * count,
            transcendentals=2 * count * ROW * ROW,
        ),
    )(ids, qkv, qkv, qkv, grads, mixed, logsum)


def pad_to(values, rows, columns):
    return jnp.pad(values, ((0, rows - values.shape[0]), (0, columns - values.shape[1])))


def lanes_up(size):
    return -(-size // LANE) * LANE


class Places:
    def __init__(self, mesh):
        self.sizes = {name: mesh.shape[name] for name in ("row", "col")}
        bits = {name: size.bit_length() - 1 for name, size in self.sizes.items()}
        self.live = [("row", b) for b in reversed(range(bits["row"]))]
        self.live += [("col", b) for b in reversed(range(bits["col"]))]
        rows = [("row", b) for b in range(bits["row"])]
        cols = [("col", b) for b in range(bits["col"])]
        self.first = rows[0]
        self.orders = (rows[1:] + cols, cols[:1] + rows[1:] + cols[1:])

    def mine(self, place):
        return (lax.axis_index(place[0]) >> place[1]) & 1

    def swap(self, values, place):
        axis, bit = place
        pairs = [(i, i ^ (1 << bit)) for i in range(self.sizes[axis])]
        return lax.ppermute(values, axis, pairs)

    def split(self, values, live, place, dim=0):
        pre = 2 ** live.index(place)
        shape = values.shape
        parts = values.reshape(shape[:dim] + (pre, 2, -1) + shape[dim + 1 :])
        half = shape[:dim] + (shape[dim] // 2,) + shape[dim + 1 :]
        mine = self.mine(place)
        send = lax.dynamic_index_in_dim(parts, 1 - mine, dim + 1, keepdims=False)
        keep = lax.dynamic_index_in_dim(parts, mine, dim + 1, keepdims=False)
        return send.reshape(half), keep.reshape(half)


def added(keep, got):
    return keep.astype(F32) + got.astype(F32)


class Chain:
    def __init__(self, places, values, order):
        self.places = places
        self.values = values
        self.live = [place for place in places.live if place != places.first]
        self.order = places.orders[order]
        self.at = 0

    def prepare(self):
        place = self.order[self.at]
        send, self.keep = self.places.split(self.values.astype(BF16), self.live, place)
        return send

    def launch(self, send):
        place = self.order[self.at]
        self.values = added(self.keep, self.places.swap(send, place))
        self.live = [other for other in self.live if other != place]
        self.at += 1

    def finish(self):
        while self.at < len(self.order):
            self.launch(self.prepare())
        return self.values


def tick(chains, *values):
    sends = tuple(chain.prepare() for chain in chains)
    held = lax.optimization_barrier((sends, values))
    for chain, send in zip(chains, held[0]):
        chain.launch(send)
    return held[1]


def halves(places, values):
    cut = lanes_up(values.shape[1] // 2)
    return [Chain(places, values[:, :cut], 0), Chain(places, values[:, cut:], 1)]


def joined(chains):
    return jnp.concatenate([chain.finish() for chain in chains], axis=1)


def solution(mesh):
    both = ("row", "col")
    devices = mesh.shape["row"] * mesh.shape["col"]
    places = Places(mesh)

    def shards(
        pixels,
        text,
        token_source,
        example_ids,
        cotangent,
        conv_weight,
        conv_bias,
        proj_weight,
        proj_bias,
        first_gain,
        query_weight,
        key_weight,
        value_weight,
        out_weight,
        second_gain,
        gate_weight,
        up_weight,
        down_weight,
    ):
        pixel_depth = pixels.shape[-1]
        vision, block = proj_weight.shape
        vision_block = conv_weight.shape[1]
        hidden_width = gate_weight.shape[1]
        pixel_lanes = lanes_up(pixel_depth + 1)

        folds = -(-vision_block // block)
        conv_local = jnp.concatenate((conv_weight.T, conv_bias[:, None]), axis=1)
        conv_local = pad_to(conv_local, folds * block, pixel_lanes)
        vectors = jnp.stack((proj_bias, first_gain, second_gain), axis=1)
        pieces = [conv_local[f * block : (f + 1) * block] for f in range(folds)]
        pieces += [proj_weight.T, pad_to(vectors, block, LANE)]
        triple = (query_weight, key_weight, value_weight)
        triple = jnp.stack([part.reshape(block, PAIRS, LANE) for part in triple], axis=2)
        pieces += [triple.reshape(block, 3 * D), out_weight.T]
        front = lax.all_gather(jnp.concatenate(pieces, axis=1), both, axis=0, tiled=True)
        ffn = lax.all_gather(
            jnp.concatenate((gate_weight, up_weight, down_weight.T), axis=1),
            both,
            axis=0,
            tiled=True,
        )
        at = folds * pixel_lanes
        conv_t = front[:, :at].reshape(devices, block, folds, pixel_lanes).transpose(0, 2, 1, 3)
        conv_t = conv_t.reshape(devices, folds * block, pixel_lanes)[:, :vision_block]
        conv_t = conv_t.reshape(devices * vision_block, pixel_lanes)
        proj_t = front[:, at : at + vision]
        at += vision
        vector_rows = front[:, at : at + LANE].T.astype(F32)
        proj_add, gain_first, gain_second = vector_rows[0], vector_rows[1], vector_rows[2]
        at += LANE
        qkv_whole = front[:, at : at + 3 * D]
        out_t = front[:, at + 3 * D :]
        gate_whole = ffn[:, :hidden_width]
        up_whole = ffn[:, hidden_width : 2 * hidden_width]
        down_t = ffn[:, 2 * hidden_width :]

        cells = pixels.reshape(-1, pixel_depth)
        ones = jnp.ones((cells.shape[0], 1), BF16)
        cells = pad_to(jnp.concatenate((cells, ones), axis=1), cells.shape[0], pixel_lanes)
        slots = lax.all_to_all(cells, both, split_axis=0, concat_axis=0, tiled=True)
        source = token_source[:, None]
        is_patch = source < PATCH_SLOTS
        pick_patch = (source == lax.iota(jnp.int32, PATCH_SLOTS)[None, :]).astype(BF16)
        text_ids = lax.iota(jnp.int32, text.shape[0]) + PATCH_SLOTS
        pick_text = (source == text_ids[None, :]).astype(BF16)
        patches = matmul(pick_patch, slots).astype(BF16)
        text_tokens = matmul(pick_text, text).astype(BF16)

        visual = right_contract(patches, conv_t).astype(BF16)
        embedded = (right_contract(visual, proj_t) + proj_add).astype(BF16)
        residual = jnp.where(is_patch, embedded, text_tokens).astype(F32)
        scale_one = lax.rsqrt(jnp.mean(residual * residual, axis=-1, keepdims=True) + 1e-06)
        normal_in = (residual * scale_one * gain_first).astype(BF16)
        qkv = matmul(normal_in, qkv_whole).astype(BF16)
        mixed, logsum = attend(qkv, example_ids)
        middle = residual + right_contract(mixed, out_t)
        scale_two = lax.rsqrt(jnp.mean(middle * middle, axis=-1, keepdims=True) + 1e-06)
        normal_mid = (middle * scale_two * gain_second).astype(BF16)
        gate = matmul(normal_mid, gate_whole)
        upward = matmul(normal_mid, up_whole)
        gate_act, gelu_pull = jax.vjp(gelu_tanh, gate)
        hidden = (gate_act * upward).astype(BF16)
        output = (middle + right_contract(hidden, down_t)).astype(BF16)

        def shares(left):
            return places.split(left, places.live, places.first, dim=1)

        def partial(left, right):
            return left_contract(left, right).astype(BF16)

        down_sum, grad_out = lax.optimization_barrier((partial(cotangent, hidden), cotangent))
        grad_hidden = matmul(grad_out, down_t)
        grad_gate = gelu_pull(grad_hidden * upward)[0].astype(BF16)
        grad_upward = (grad_hidden * gate_act).astype(BF16)
        ffn_sums = (partial(normal_mid, grad_gate), partial(normal_mid, grad_upward), down_sum)
        ffn_sums, grad_gate, grad_upward = lax.optimization_barrier(
            (jnp.concatenate(ffn_sums, axis=1), grad_gate, grad_upward)
        )
        ffn_sums = lax.psum_scatter(ffn_sums, both, scatter_dimension=0, tiled=True).astype(F32)
        grad_mid = right_contract(grad_gate, gate_whole) + right_contract(grad_upward, up_whole)
        gain_two_sum = jnp.sum(grad_mid * middle * scale_two, axis=0)
        pulled = grad_mid * gain_second
        pulled_mean = jnp.mean(pulled * middle, axis=-1, keepdims=True)
        grad_middle = cotangent.astype(F32) + scale_two * (
            pulled - middle * (scale_two * scale_two) * pulled_mean
        )
        grad_branch = grad_middle.astype(BF16)

        theirs, ours = shares(grad_branch)
        grad_mixed = matmul(grad_branch, out_t).astype(BF16)
        out_send, grad_mixed = lax.optimization_barrier((partial(theirs, mixed), grad_mixed))
        out_sum = added(partial(ours, mixed), places.swap(out_send, places.first))
        theirs, ours = shares(normal_in)
        cut = PAIRS // 2

        def back(grads, start):
            return attend_back(qkv, grads, mixed, logsum, example_ids, start, PAIRS - cut)

        early = back(grad_mixed, 0)
        early_send, grad_mixed = lax.optimization_barrier((partial(theirs, early), grad_mixed))
        early_sum = added(partial(ours, early), places.swap(early_send, places.first))
        one = halves(places, jnp.concatenate((early_sum, out_sum), axis=1))
        early, grad_mixed = tick(one, early, grad_mixed)
        late = back(grad_mixed, cut)
        late_send, late = tick(one, partial(theirs, late), late)

        late_got = places.swap(late_send, places.first)
        at = early.shape[1]
        grad_normal = right_contract(early, qkv_whole[:, :at])
        grad_normal += right_contract(late, qkv_whole[:, at:])
        two = halves(places, added(partial(ours, late), late_got))
        (grad_normal,) = tick(one + two, grad_normal)
        gain_one_sum = jnp.sum(grad_normal * residual * scale_one, axis=0)
        pulled = grad_normal * gain_first
        pulled_mean = jnp.mean(pulled * residual, axis=-1, keepdims=True)
        grad_residual = grad_middle + scale_one * (
            pulled - residual * (scale_one * scale_one) * pulled_mean
        )

        grad_embedded = jnp.where(is_patch, grad_residual, 0.0).astype(BF16)
        proj_add_sum = jnp.sum(grad_embedded.astype(F32), axis=0)
        sums = jnp.stack((proj_add_sum, gain_one_sum, gain_two_sum), axis=0)
        sums_send, sums_keep = places.split(
            pad_to(sums, LANE, D).T.astype(BF16), places.live, places.first
        )
        theirs, ours = shares(grad_embedded)
        proj_send = jnp.concatenate((partial(theirs, visual), sums_send), axis=1)
        proj_send, grad_embedded = tick(one + two, proj_send, grad_embedded)
        proj_got = places.swap(proj_send, places.first)
        grad_visual = matmul(grad_embedded, proj_t).astype(BF16)
        conv_send, conv_keep = places.split(
            partial(grad_visual, patches), places.live, places.first
        )
        conv_send, grad_visual = tick(two, conv_send, grad_visual)
        conv_got = places.swap(conv_send, places.first)
        grad_patches = matmul(grad_visual, conv_t).astype(BF16)
        grad_slots = left_contract(pick_patch, grad_patches).astype(BF16)
        grad_cells = lax.all_to_all(grad_slots, both, split_axis=0, concat_axis=0, tiled=True)
        grad_pixels = grad_cells[:, :pixel_depth].astype(F32).reshape(pixels.shape)
        proj_sum = jnp.concatenate((partial(ours, visual), sums_keep), axis=1)
        conv_sum = added(conv_keep, conv_got).astype(BF16)
        conv_sum = conv_sum.reshape(-1, vision_block, pixel_lanes)
        conv_sum = jnp.pad(conv_sum, ((0, 0), (0, folds * block - vision_block), (0, 0)))
        conv_sum = conv_sum.reshape(-1, folds, block, pixel_lanes).transpose(0, 2, 1, 3)
        conv_sum = conv_sum.reshape(-1, folds * pixel_lanes)
        proj_sum = added(proj_sum, proj_got).astype(BF16)
        three = joined(halves(places, jnp.concatenate((proj_sum, conv_sum), axis=1)))
        one, two = joined(one), joined(two)
        at = early_sum.shape[1]
        grad_qkv = jnp.concatenate((one[:, :at], two), axis=1).reshape(block, PAIRS, 3, LANE)
        grad_query, grad_key, grad_value = [
            grad_qkv[:, :, k].reshape(block, D) for k in range(3)
        ]
        grad_proj_t, sums = three[:, :vision], three[:, vision : vision + LANE]
        grad_conv_t = three[:, vision + LANE :].reshape(block, folds, pixel_lanes)
        grad_conv_t = grad_conv_t.transpose(1, 0, 2).reshape(folds * block, pixel_lanes)
        grad_conv_t = grad_conv_t[:vision_block]
        return (
            output,
            grad_pixels,
            grad_conv_t[:, :pixel_depth].T,
            grad_conv_t[:, pixel_depth],
            grad_proj_t.T,
            sums[:, 0],
            sums[:, 1],
            grad_query,
            grad_key,
            grad_value,
            one[:, at:].T,
            sums[:, 2],
            ffn_sums[:, :hidden_width],
            ffn_sums[:, hidden_width : 2 * hidden_width],
            ffn_sums[:, 2 * hidden_width :].T,
        )

    rows = P(both, None)
    columns = P(None, both)
    vector = P(both)
    tiles = P("row", "col", None)
    return jax.shard_map(
        shards,
        mesh=mesh,
        in_specs=(
            tiles,
            rows,
            vector,
            vector,
            rows,
            columns,
            vector,
            columns,
            vector,
            vector,
            rows,
            rows,
            rows,
            columns,
            vector,
            rows,
            rows,
            columns,
        ),
        out_specs=(
            rows,
            tiles,
            columns,
            vector,
            columns,
            vector,
            vector,
            rows,
            rows,
            rows,
            columns,
            vector,
            rows,
            rows,
            columns,
        ),
        check_vma=False,
    )
```

```python
import jax
import jax.numpy as jnp
from jax import lax
from jax.experimental import pallas as pl
from jax.experimental.pallas import tpu as pltpu
from jax.sharding import PartitionSpec as P

D = 1024
H = 16
HD = 64
PATCH_SLOTS = 1024
ROW = 1152
SPAN = 384
LANE = 128
PAIRS = D // LANE
F32 = jnp.float32
BF16 = jnp.bfloat16


def gelu_tanh(values):
    return jax.nn.gelu(values, approximate=True)


def matmul(left, right):
    return jnp.dot(left, right, preferred_element_type=F32)


def left_contract(left, right):
    return lax.dot_general(left, right, (((0,), (0,)), ((), ())), preferred_element_type=F32)


def right_contract(left, right):
    return lax.dot_general(left, right, (((1,), (1,)), ((), ())), preferred_element_type=F32)


def low_lanes(rows):
    return lax.broadcasted_iota(jnp.int32, (rows, LANE), 1) < HD


def attend_kernel(ids_ref, q_ref, k_ref, v_ref, o_ref, l_ref):
    single = ids_ref[0] == ids_ref[ROW - 1]

    def tile(t, base, keys):
        at = pl.ds(pl.multiple_of(t * SPAN, SPAN), SPAN)
        query = q_ref[at, :] * 0.125
        key = k_ref[pl.ds(base, keys), :]
        value = v_ref[pl.ds(base, keys), :]
        low, low_keys = low_lanes(SPAN), low_lanes(keys)
        mixes, tops = [], []
        for h in range(2):
            mine = low if h == 0 else ~low
            mine_keys = low_keys if h == 0 else ~low_keys
            scores = right_contract(jnp.where(mine, query, jnp.zeros_like(query)), key)
            top = jnp.max(scores, axis=-1, keepdims=True)
            powers = jnp.exp(scores - top).astype(BF16)
            mixes.append(matmul(powers, jnp.where(mine_keys, value, jnp.ones_like(value))))
            tops.append(top)
        total = pltpu.roll(jnp.where(low, mixes[1], mixes[0]), HD, 1)
        o_ref[at, :] = (jnp.where(low, mixes[0], mixes[1]) / total).astype(BF16)
        logs = (jnp.where(low, tops[0], tops[1]) + jnp.log(total)).T
        l_ref[0, :, at] = jnp.concatenate([logs[0:8], logs[HD : HD + 8]], axis=0)

    @pl.when(single)
    def _():
        lax.fori_loop(0, ROW // SPAN, lambda t, c: (tile(t, 0, ROW), c)[1], 0)

    @pl.when(jnp.logical_not(single))
    def _():
        def body(t, c):
            tile(t, pl.multiple_of(t * SPAN, SPAN), SPAN)
            return c

        lax.fori_loop(0, ROW // SPAN, body, 0)


def attend(qkv, ids):
    def part(which):
        return pl.BlockSpec((ROW, LANE), lambda i, ids: (0, 3 * i + which))

    return pl.pallas_call(
        attend_kernel,
        out_shape=(
            jax.ShapeDtypeStruct((ROW, D), BF16),
            jax.ShapeDtypeStruct((PAIRS, 16, ROW), F32),
        ),
        grid_spec=pltpu.PrefetchScalarGridSpec(
            num_scalar_prefetch=1,
            grid=(PAIRS,),
            in_specs=[part(0), part(1), part(2)],
            out_specs=[pl.BlockSpec((ROW, LANE), lambda i, ids: (0, i)), pl.BlockSpec((1, 16, ROW), lambda i, ids: (i, 0, 0))],
        ),
        compiler_params=pltpu.CompilerParams(vmem_limit_bytes=40 << 20),
        cost_estimate=pl.CostEstimate(
            flops=16 * ROW * ROW * D, bytes_accessed=8 * ROW * D, transcendentals=H * ROW * ROW
        ),
    )(ids, qkv, qkv, qkv)


def back_kernel(ids_ref, q_ref, k_ref, v_ref, g_ref, o_ref, l_ref, d_ref, key_sum, value_sum):
    single = ids_ref[0] == ids_ref[ROW - 1]

    def tile(t, base, keys, first):
        at = pl.ds(pl.multiple_of(t * SPAN, SPAN), SPAN)
        from_keys = pl.ds(base, keys)
        query, grad = q_ref[at, :] * 0.125, g_ref[at, :]
        key, value = k_ref[from_keys, :], v_ref[from_keys, :]
        low = low_lanes(SPAN)
        blank = jnp.zeros_like(query)
        products = grad.astype(F32) * o_ref[at, :].astype(F32)
        row_head = lax.broadcasted_iota(jnp.int32, (16, LANE), 0) // 8
        lane_head = lax.broadcasted_iota(jnp.int32, (16, LANE), 1) // HD
        delta = lax.dot_general(
            (row_head == lane_head).astype(F32),
            products,
            (((1,), (1,)), ((), ())),
            preferred_element_type=F32,
            precision=lax.Precision.HIGHEST,
        )
        key_t = key.T
        grad_query, grad_key, grad_value = [], 0.0, 0.0
        for h in range(2):
            mine = low if h == 0 else ~low
            query_h, grad_h = jnp.where(mine, query, blank), jnp.where(mine, grad, blank)
            chances = jnp.exp(right_contract(key, query_h) - l_ref[0, 8 * h : 8 * h + 1, at])
            grad_chances = right_contract(value, grad_h)
            grad_scores = (chances * (grad_chances - delta[8 * h : 8 * h + 1, :])).astype(BF16)
            grad_query.append(matmul(key_t[h * HD : (h + 1) * HD, :], grad_scores))
            grad_value += matmul(chances.astype(BF16), grad_h)
            grad_key += matmul(grad_scores, query_h)
        d_ref[at, :LANE] = (jnp.concatenate(grad_query, axis=0) * 0.125).T.astype(BF16)
        if first is None:
            d_ref[from_keys, LANE : 2 * LANE] = grad_key.astype(BF16)
            d_ref[from_keys, 2 * LANE :] = grad_value.astype(BF16)
            return

        @pl.when(first)
        def _():
            key_sum[...] = grad_key
            value_sum[...] = grad_value

        @pl.when(jnp.logical_not(first))
        def _():
            key_sum[...] += grad_key
            value_sum[...] += grad_value

    @pl.when(single)
    def _():
        lax.fori_loop(0, ROW // SPAN, lambda t, c: (tile(t, 0, ROW, t == 0), c)[1], 0)
        d_ref[:, LANE : 2 * LANE] = key_sum[...].astype(BF16)
        d_ref[:, 2 * LANE :] = value_sum[...].astype(BF16)

    @pl.when(jnp.logical_not(single))
    def _():
        def body(t, c):
            tile(t, pl.multiple_of(t * SPAN, SPAN), SPAN, None)
            return c

        lax.fori_loop(0, ROW // SPAN, body, 0)


def attend_back(qkv, grads, mixed, logsum, ids, start, count):
    def part(which):
        return pl.BlockSpec((ROW, LANE), lambda i, ids: (0, 3 * (start + i) + which))

    pair = pl.BlockSpec((ROW, LANE), lambda i, ids: (0, start + i))
    logs = pl.BlockSpec((1, 16, ROW), lambda i, ids: (start + i, 0, 0))
    return pl.pallas_call(
        back_kernel,
        out_shape=jax.ShapeDtypeStruct((ROW, 3 * LANE * count), BF16),
        grid_spec=pltpu.PrefetchScalarGridSpec(
            num_scalar_prefetch=1,
            grid=(count,),
            in_specs=[part(0), part(1), part(2), pair, pair, logs],
            out_specs=pl.BlockSpec((ROW, 3 * LANE), lambda i, ids: (0, i)),
            scratch_shapes=[pltpu.VMEM((ROW, LANE), F32)] * 2,
        ),
        compiler_params=pltpu.CompilerParams(vmem_limit_bytes=40 << 20),
        cost_estimate=pl.CostEstimate(
            flops=40 * ROW * ROW * LANE * count,
            bytes_accessed=16 * ROW * LANE * count,
            transcendentals=2 * count * ROW * ROW,
        ),
    )(ids, qkv, qkv, qkv, grads, mixed, logsum)


def weights_kernel(mid_ref, out_ref, gate_ref, up_ref, hidden_ref, sum_ref, left):
    step = pl.program_id(0)

    @pl.when(step == 0)
    def _():
        left[...] = mid_ref[...].T

    @pl.when(step == 4)
    def _():
        left[...] = out_ref[...].T

    rows = 256

    def product(right_ref):
        def body(k, c):
            at = pl.ds(pl.multiple_of(k * rows, rows), rows)
            sum_ref[at, :] = matmul(left[at, :], right_ref[...]).astype(BF16)
            return c

        lax.fori_loop(0, D // rows, body, 0)

    for k, right_ref in enumerate((gate_ref, up_ref, hidden_ref)):
        pl.when(step // 2 == k)(lambda right_ref=right_ref: product(right_ref))


def weight_sums(normal_mid, grad_out, grad_gate, grad_upward, hidden):
    tokens, width = hidden.shape
    half = width // 2
    whole = pl.BlockSpec((tokens, D), lambda s: (0, 0), pipeline_mode=pl.Buffered(1))

    def columns(first):
        return pl.BlockSpec((tokens, half), lambda s: (0, jnp.clip(s - first, 0, 1)))

    return pl.pallas_call(
        weights_kernel,
        out_shape=jax.ShapeDtypeStruct((D, 3 * width), BF16),
        grid_spec=pltpu.PrefetchScalarGridSpec(
            num_scalar_prefetch=0,
            grid=(6,),
            in_specs=[whole, whole, columns(0), columns(2), columns(4)],
            out_specs=pl.BlockSpec((D, half), lambda s: (0, s)),
            scratch_shapes=[pltpu.VMEM((D, tokens), BF16)],
        ),
        compiler_params=pltpu.CompilerParams(vmem_limit_bytes=48 << 20),
        cost_estimate=pl.CostEstimate(
            flops=6 * tokens * D * width, bytes_accessed=6 * width * (tokens + D), transcendentals=0
        ),
    )(normal_mid, grad_out, grad_gate, grad_upward, hidden)


def pad_to(values, rows, columns):
    return jnp.pad(values, ((0, rows - values.shape[0]), (0, columns - values.shape[1])))


def lanes_up(size):
    return -(-size // LANE) * LANE


class Places:
    def __init__(self, mesh):
        self.sizes = {name: mesh.shape[name] for name in ("row", "col")}
        bits = {name: size.bit_length() - 1 for name, size in self.sizes.items()}
        self.live = [("row", b) for b in reversed(range(bits["row"]))]
        self.live += [("col", b) for b in reversed(range(bits["col"]))]
        rows = [("row", b) for b in range(bits["row"])]
        cols = [("col", b) for b in range(bits["col"])]
        self.first = rows[0]
        self.orders = (rows[1:] + cols, cols[:1] + rows[1:] + cols[1:])

    def mine(self, place):
        return (lax.axis_index(place[0]) >> place[1]) & 1

    def swap(self, values, place):
        axis, bit = place
        pairs = [(i, i ^ (1 << bit)) for i in range(self.sizes[axis])]
        return lax.ppermute(values, axis, pairs)

    def split(self, values, live, place, dim=0):
        pre = 2 ** live.index(place)
        shape = values.shape
        parts = values.reshape(shape[:dim] + (pre, 2, -1) + shape[dim + 1 :])
        half = shape[:dim] + (shape[dim] // 2,) + shape[dim + 1 :]
        mine = self.mine(place)
        send = lax.dynamic_index_in_dim(parts, 1 - mine, dim + 1, keepdims=False)
        keep = lax.dynamic_index_in_dim(parts, mine, dim + 1, keepdims=False)
        return send.reshape(half), keep.reshape(half)


def added(keep, got):
    return keep.astype(F32) + got.astype(F32)


class Chain:
    def __init__(self, places, values, order):
        self.places = places
        self.values = values
        self.live = [place for place in places.live if place != places.first]
        self.order = places.orders[order]
        self.at = 0

    def prepare(self):
        place = self.order[self.at]
        send, self.keep = self.places.split(self.values.astype(BF16), self.live, place)
        return send

    def launch(self, send):
        place = self.order[self.at]
        self.values = added(self.keep, self.places.swap(send, place))
        self.live = [other for other in self.live if other != place]
        self.at += 1

    def finish(self):
        while self.at < len(self.order):
            self.launch(self.prepare())
        return self.values


def tick(chains, *values):
    sends = tuple(chain.prepare() for chain in chains)
    held = lax.optimization_barrier((sends, values))
    for chain, send in zip(chains, held[0]):
        chain.launch(send)
    return held[1]


def halves(places, values):
    cut = lanes_up(values.shape[1] // 2)
    return [Chain(places, values[:, :cut], 0), Chain(places, values[:, cut:], 1)]


def joined(chains):
    return jnp.concatenate([chain.finish() for chain in chains], axis=1)


def solution(mesh):
    both = ("row", "col")
    devices = mesh.shape["row"] * mesh.shape["col"]
    places = Places(mesh)

    def shards(
        pixels,
        text,
        token_source,
        example_ids,
        cotangent,
        conv_weight,
        conv_bias,
        proj_weight,
        proj_bias,
        first_gain,
        query_weight,
        key_weight,
        value_weight,
        out_weight,
        second_gain,
        gate_weight,
        up_weight,
        down_weight,
    ):
        pixel_depth = pixels.shape[-1]
        vision, block = proj_weight.shape
        vision_block = conv_weight.shape[1]
        hidden_width = gate_weight.shape[1]
        pixel_lanes = lanes_up(pixel_depth + 1)

        folds = -(-vision_block // block)
        conv_local = jnp.concatenate((conv_weight.T, conv_bias[:, None]), axis=1)
        conv_local = pad_to(conv_local, folds * block, pixel_lanes)
        vectors = jnp.stack((proj_bias, first_gain, second_gain), axis=1)
        pieces = [conv_local[f * block : (f + 1) * block] for f in range(folds)]
        pieces += [proj_weight.T, pad_to(vectors, block, LANE)]
        triple = (query_weight, key_weight, value_weight)
        triple = jnp.stack([part.reshape(block, PAIRS, LANE) for part in triple], axis=2)
        pieces += [triple.reshape(block, 3 * D), out_weight.T]
        front = lax.all_gather(jnp.concatenate(pieces, axis=1), both, axis=0, tiled=True)
        ffn = lax.all_gather(
            jnp.concatenate((gate_weight, up_weight, down_weight.T), axis=1),
            both,
            axis=0,
            tiled=True,
        )
        at = folds * pixel_lanes
        conv_t = front[:, :at].reshape(devices, block, folds, pixel_lanes).transpose(0, 2, 1, 3)
        conv_t = conv_t.reshape(devices, folds * block, pixel_lanes)[:, :vision_block]
        conv_t = conv_t.reshape(devices * vision_block, pixel_lanes)
        proj_t = front[:, at : at + vision]
        at += vision
        vector_rows = front[:, at : at + LANE].T.astype(F32)
        proj_add, gain_first, gain_second = vector_rows[0], vector_rows[1], vector_rows[2]
        at += LANE
        qkv_whole = front[:, at : at + 3 * D]
        out_t = front[:, at + 3 * D :]
        gate_whole = ffn[:, :hidden_width]
        up_whole = ffn[:, hidden_width : 2 * hidden_width]
        down_t = ffn[:, 2 * hidden_width :]

        cells = pixels.reshape(-1, pixel_depth)
        ones = jnp.ones((cells.shape[0], 1), BF16)
        cells = pad_to(jnp.concatenate((cells, ones), axis=1), cells.shape[0], pixel_lanes)
        slots = lax.all_to_all(cells, both, split_axis=0, concat_axis=0, tiled=True)
        source = token_source[:, None]
        is_patch = source < PATCH_SLOTS
        pick_patch = (source == lax.iota(jnp.int32, PATCH_SLOTS)[None, :]).astype(BF16)
        text_ids = lax.iota(jnp.int32, text.shape[0]) + PATCH_SLOTS
        pick_text = (source == text_ids[None, :]).astype(BF16)
        patches = matmul(pick_patch, slots).astype(BF16)
        text_tokens = matmul(pick_text, text).astype(BF16)

        visual = right_contract(patches, conv_t).astype(BF16)
        embedded = (right_contract(visual, proj_t) + proj_add).astype(BF16)
        residual = jnp.where(is_patch, embedded, text_tokens).astype(F32)
        scale_one = lax.rsqrt(jnp.mean(residual * residual, axis=-1, keepdims=True) + 1e-06)
        normal_in = (residual * scale_one * gain_first).astype(BF16)
        qkv = matmul(normal_in, qkv_whole).astype(BF16)
        mixed, logsum = attend(qkv, example_ids)
        middle = residual + right_contract(mixed, out_t)
        scale_two = lax.rsqrt(jnp.mean(middle * middle, axis=-1, keepdims=True) + 1e-06)
        normal_mid = (middle * scale_two * gain_second).astype(BF16)
        gate = matmul(normal_mid, gate_whole)
        upward = matmul(normal_mid, up_whole)
        gate_act, gelu_pull = jax.vjp(gelu_tanh, gate)
        hidden = (gate_act * upward).astype(BF16)
        output = (middle + right_contract(hidden, down_t)).astype(BF16)

        def shares(left):
            return places.split(left, places.live, places.first, dim=1)

        def partial(left, right):
            return left_contract(left, right).astype(BF16)

        grad_hidden = matmul(cotangent, down_t)
        grad_gate = gelu_pull(grad_hidden * upward)[0].astype(BF16)
        grad_upward = (grad_hidden * gate_act).astype(BF16)
        ffn_sums, grad_gate, grad_upward = lax.optimization_barrier(
            (
                weight_sums(normal_mid, cotangent, grad_gate, grad_upward, hidden),
                grad_gate,
                grad_upward,
            )
        )
        ffn_sums = lax.psum_scatter(ffn_sums, both, scatter_dimension=0, tiled=True).astype(F32)
        grad_mid = right_contract(grad_gate, gate_whole) + right_contract(grad_upward, up_whole)
        gain_two_sum = jnp.sum(grad_mid * middle * scale_two, axis=0)
        pulled = grad_mid * gain_second
        pulled_mean = jnp.mean(pulled * middle, axis=-1, keepdims=True)
        grad_middle = cotangent.astype(F32) + scale_two * (
            pulled - middle * (scale_two * scale_two) * pulled_mean
        )
        grad_branch = grad_middle.astype(BF16)

        theirs, ours = shares(grad_branch)
        grad_mixed = matmul(grad_branch, out_t).astype(BF16)
        out_send, grad_mixed = lax.optimization_barrier((partial(theirs, mixed), grad_mixed))
        out_sum = added(partial(ours, mixed), places.swap(out_send, places.first))
        theirs, ours = shares(normal_in)
        cut = PAIRS // 2

        def back(grads, start):
            return attend_back(qkv, grads, mixed, logsum, example_ids, start, PAIRS - cut)

        early = back(grad_mixed, 0)
        early_send, grad_mixed = lax.optimization_barrier((partial(theirs, early), grad_mixed))
        early_sum = added(partial(ours, early), places.swap(early_send, places.first))
        one = halves(places, jnp.concatenate((early_sum, out_sum), axis=1))
        early, grad_mixed = tick(one, early, grad_mixed)
        late = back(grad_mixed, cut)
        late_send, late = tick(one, partial(theirs, late), late)

        late_got = places.swap(late_send, places.first)
        at = early.shape[1]
        grad_normal = right_contract(early, qkv_whole[:, :at])
        grad_normal += right_contract(late, qkv_whole[:, at:])
        two = halves(places, added(partial(ours, late), late_got))
        (grad_normal,) = tick(one + two, grad_normal)
        gain_one_sum = jnp.sum(grad_normal * residual * scale_one, axis=0)
        pulled = grad_normal * gain_first
        pulled_mean = jnp.mean(pulled * residual, axis=-1, keepdims=True)
        grad_residual = grad_middle + scale_one * (
            pulled - residual * (scale_one * scale_one) * pulled_mean
        )

        grad_embedded = jnp.where(is_patch, grad_residual, 0.0).astype(BF16)
        proj_add_sum = jnp.sum(grad_embedded.astype(F32), axis=0)
        sums = jnp.stack((proj_add_sum, gain_one_sum, gain_two_sum), axis=0)
        sums_send, sums_keep = places.split(
            pad_to(sums, LANE, D).T.astype(BF16), places.live, places.first
        )
        theirs, ours = shares(grad_embedded)
        proj_send = jnp.concatenate((partial(theirs, visual), sums_send), axis=1)
        proj_send, grad_embedded = tick(one + two, proj_send, grad_embedded)
        proj_got = places.swap(proj_send, places.first)
        grad_visual = matmul(grad_embedded, proj_t).astype(BF16)
        conv_send, conv_keep = places.split(
            partial(grad_visual, patches), places.live, places.first
        )
        conv_send, grad_visual = tick(two, conv_send, grad_visual)
        conv_got = places.swap(conv_send, places.first)
        grad_patches = matmul(grad_visual, conv_t).astype(BF16)
        slot_ids = lax.iota(jnp.int32, PATCH_SLOTS)[:, None]
        named = (slot_ids == token_source[None, :]).astype(BF16)
        grad_slots = matmul(named, grad_patches).astype(BF16)
        grad_cells = lax.all_to_all(grad_slots, both, split_axis=0, concat_axis=0, tiled=True)
        grad_pixels = grad_cells[:, :pixel_depth].astype(F32).reshape(pixels.shape)
        proj_sum = jnp.concatenate((partial(ours, visual), sums_keep), axis=1)
        conv_sum = added(conv_keep, conv_got).astype(BF16)
        conv_sum = conv_sum.reshape(-1, vision_block, pixel_lanes)
        conv_sum = jnp.pad(conv_sum, ((0, 0), (0, folds * block - vision_block), (0, 0)))
        conv_sum = conv_sum.reshape(-1, folds, block, pixel_lanes).transpose(0, 2, 1, 3)
        conv_sum = conv_sum.reshape(-1, folds * pixel_lanes)
        proj_sum = added(proj_sum, proj_got).astype(BF16)
        three = joined(halves(places, jnp.concatenate((proj_sum, conv_sum), axis=1)))
        one, two = joined(one), joined(two)
        at = early_sum.shape[1]
        grad_qkv = jnp.concatenate((one[:, :at], two), axis=1).reshape(block, PAIRS, 3, LANE)
        grad_query, grad_key, grad_value = [
            grad_qkv[:, :, k].reshape(block, D) for k in range(3)
        ]
        grad_proj_t, sums = three[:, :vision], three[:, vision : vision + LANE]
        grad_conv_t = three[:, vision + LANE :].reshape(block, folds, pixel_lanes)
        grad_conv_t = grad_conv_t.transpose(1, 0, 2).reshape(folds * block, pixel_lanes)
        grad_conv_t = grad_conv_t[:vision_block]
        return (
            output,
            grad_pixels,
            grad_conv_t[:, :pixel_depth].T,
            grad_conv_t[:, pixel_depth],
            grad_proj_t.T,
            sums[:, 0],
            sums[:, 1],
            grad_query,
            grad_key,
            grad_value,
            one[:, at:].T,
            sums[:, 2],
            ffn_sums[:, :hidden_width],
            ffn_sums[:, hidden_width : 2 * hidden_width],
            ffn_sums[:, 2 * hidden_width :].T,
        )

    rows = P(both, None)
    columns = P(None, both)
    vector = P(both)
    tiles = P("row", "col", None)
    return jax.shard_map(
        shards,
        mesh=mesh,
        in_specs=(
            tiles,
            rows,
            vector,
            vector,
            rows,
            columns,
            vector,
            columns,
            vector,
            vector,
            rows,
            rows,
            rows,
            columns,
            vector,
            rows,
            rows,
            columns,
        ),
        out_specs=(
            rows,
            tiles,
            columns,
            vector,
            columns,
            vector,
            vector,
            rows,
            rows,
            rows,
            columns,
            vector,
            rows,
            rows,
            columns,
        ),
        check_vma=False,
    )
```

```python
import jax
import jax.numpy as jnp
from jax import lax
from jax.experimental import pallas as pl
from jax.experimental.pallas import tpu as pltpu
from jax.sharding import PartitionSpec as P


D = 1024
H = 16
HD = 64
PATCH_SLOTS = 1024
ROW = 1152
SPAN = 384
LANE = 128
PAIRS = D // LANE
F32 = jnp.float32
BF16 = jnp.bfloat16


def gelu_tanh(values):
    return jax.nn.gelu(values, approximate=True)


def matmul(left, right):
    return jnp.dot(left, right, preferred_element_type=F32)


def left_contract(left, right):
    return lax.dot_general(left, right, (((0,), (0,)), ((), ())), preferred_element_type=F32)


def right_contract(left, right):
    return lax.dot_general(left, right, (((1,), (1,)), ((), ())), preferred_element_type=F32)


def low_lanes(rows):
    return lax.broadcasted_iota(jnp.int32, (rows, LANE), 1) < HD


def attend_kernel(ids_ref, q_ref, k_ref, v_ref, o_ref, l_ref):
    single = ids_ref[0] == ids_ref[ROW - 1]

    def tile(t, base, keys):
        at = pl.ds(pl.multiple_of(t * SPAN, SPAN), SPAN)
        query = q_ref[at, :] * 0.125
        key = k_ref[pl.ds(base, keys), :]
        value = v_ref[pl.ds(base, keys), :]
        low, low_keys = low_lanes(SPAN), low_lanes(keys)
        mixes, tops = [], []
        for h in range(2):
            mine = low if h == 0 else ~low
            mine_keys = low_keys if h == 0 else ~low_keys
            scores = right_contract(jnp.where(mine, query, jnp.zeros_like(query)), key)
            top = jnp.max(scores, axis=-1, keepdims=True)
            powers = jnp.exp(scores - top).astype(BF16)
            mixes.append(matmul(powers, jnp.where(mine_keys, value, jnp.ones_like(value))))
            tops.append(top)
        total = pltpu.roll(jnp.where(low, mixes[1], mixes[0]), HD, 1)
        o_ref[at, :] = (jnp.where(low, mixes[0], mixes[1]) / total).astype(BF16)
        logs = (jnp.where(low, tops[0], tops[1]) + jnp.log(total)).T
        l_ref[0, :, at] = jnp.concatenate([logs[0:8], logs[HD : HD + 8]], axis=0)

    @pl.when(single)
    def _():
        lax.fori_loop(0, ROW // SPAN, lambda t, c: (tile(t, 0, ROW), c)[1], 0)

    @pl.when(jnp.logical_not(single))
    def _():
        def body(t, c):
            tile(t, pl.multiple_of(t * SPAN, SPAN), SPAN)
            return c

        lax.fori_loop(0, ROW // SPAN, body, 0)


def attend(qkv, ids):
    def part(which):
        return pl.BlockSpec((ROW, LANE), lambda i, ids: (0, 3 * i + which))

    return pl.pallas_call(
        attend_kernel,
        out_shape=(
            jax.ShapeDtypeStruct((ROW, D), BF16),
            jax.ShapeDtypeStruct((PAIRS, 16, ROW), F32),
        ),
        grid_spec=pltpu.PrefetchScalarGridSpec(
            num_scalar_prefetch=1,
            grid=(PAIRS,),
            in_specs=[part(0), part(1), part(2)],
            out_specs=[pl.BlockSpec((ROW, LANE), lambda i, ids: (0, i)), pl.BlockSpec((1, 16, ROW), lambda i, ids: (i, 0, 0))],
        ),
        compiler_params=pltpu.CompilerParams(vmem_limit_bytes=40 << 20),
        cost_estimate=pl.CostEstimate(
            flops=16 * ROW * ROW * D, bytes_accessed=8 * ROW * D, transcendentals=H * ROW * ROW
        ),
    )(ids, qkv, qkv, qkv)


def back_kernel(ids_ref, q_ref, k_ref, v_ref, g_ref, o_ref, l_ref, d_ref, key_sum, value_sum):
    single = ids_ref[0] == ids_ref[ROW - 1]

    def tile(t, base, keys, first):
        at = pl.ds(pl.multiple_of(t * SPAN, SPAN), SPAN)
        from_keys = pl.ds(base, keys)
        query, grad = q_ref[at, :] * 0.125, g_ref[at, :]
        key, value = k_ref[from_keys, :], v_ref[from_keys, :]
        low = low_lanes(SPAN)
        blank = jnp.zeros_like(query)
        products = grad.astype(F32) * o_ref[at, :].astype(F32)
        row_head = lax.broadcasted_iota(jnp.int32, (16, LANE), 0) // 8
        lane_head = lax.broadcasted_iota(jnp.int32, (16, LANE), 1) // HD
        delta = lax.dot_general(
            (row_head == lane_head).astype(F32),
            products,
            (((1,), (1,)), ((), ())),
            preferred_element_type=F32,
            precision=lax.Precision.HIGHEST,
        )
        key_t = key.T
        grad_query, grad_key, grad_value = [], 0.0, 0.0
        for h in range(2):
            mine = low if h == 0 else ~low
            query_h, grad_h = jnp.where(mine, query, blank), jnp.where(mine, grad, blank)
            chances = jnp.exp(right_contract(key, query_h) - l_ref[0, 8 * h : 8 * h + 1, at])
            grad_chances = right_contract(value, grad_h)
            grad_scores = (chances * (grad_chances - delta[8 * h : 8 * h + 1, :])).astype(BF16)
            grad_query.append(matmul(key_t[h * HD : (h + 1) * HD, :], grad_scores))
            grad_value += matmul(chances.astype(BF16), grad_h)
            grad_key += matmul(grad_scores, query_h)
        d_ref[at, :LANE] = (jnp.concatenate(grad_query, axis=0) * 0.125).T.astype(BF16)
        if first is None:
            d_ref[from_keys, LANE : 2 * LANE] = grad_key.astype(BF16)
            d_ref[from_keys, 2 * LANE :] = grad_value.astype(BF16)
            return

        @pl.when(first)
        def _():
            key_sum[...] = grad_key
            value_sum[...] = grad_value

        @pl.when(jnp.logical_not(first))
        def _():
            key_sum[...] += grad_key
            value_sum[...] += grad_value

    @pl.when(single)
    def _():
        lax.fori_loop(0, ROW // SPAN, lambda t, c: (tile(t, 0, ROW, t == 0), c)[1], 0)
        d_ref[:, LANE : 2 * LANE] = key_sum[...].astype(BF16)
        d_ref[:, 2 * LANE :] = value_sum[...].astype(BF16)

    @pl.when(jnp.logical_not(single))
    def _():
        def body(t, c):
            tile(t, pl.multiple_of(t * SPAN, SPAN), SPAN, None)
            return c

        lax.fori_loop(0, ROW // SPAN, body, 0)


def attend_back(qkv, grads, mixed, logsum, ids, start, count):
    def part(which):
        return pl.BlockSpec((ROW, LANE), lambda i, ids: (0, 3 * (start + i) + which))

    pair = pl.BlockSpec((ROW, LANE), lambda i, ids: (0, start + i))
    logs = pl.BlockSpec((1, 16, ROW), lambda i, ids: (start + i, 0, 0))
    return pl.pallas_call(
        back_kernel,
        out_shape=jax.ShapeDtypeStruct((ROW, 3 * LANE * count), BF16),
        grid_spec=pltpu.PrefetchScalarGridSpec(
            num_scalar_prefetch=1,
            grid=(count,),
            in_specs=[part(0), part(1), part(2), pair, pair, logs],
            out_specs=pl.BlockSpec((ROW, 3 * LANE), lambda i, ids: (0, i)),
            scratch_shapes=[pltpu.VMEM((ROW, LANE), F32)] * 2,
        ),
        compiler_params=pltpu.CompilerParams(vmem_limit_bytes=40 << 20),
        cost_estimate=pl.CostEstimate(
            flops=40 * ROW * ROW * LANE * count,
            bytes_accessed=16 * ROW * LANE * count,
            transcendentals=2 * count * ROW * ROW,
        ),
    )(ids, qkv, qkv, qkv, grads, mixed, logsum)


def weights_kernel(mid_ref, out_ref, gate_ref, up_ref, hidden_ref, sum_ref, left):
    step = pl.program_id(0)

    @pl.when(step == 0)
    def _():
        left[...] = mid_ref[...].T

    @pl.when(step == 4)
    def _():
        left[...] = out_ref[...].T

    rows = 256

    def product(right_ref):
        def body(k, c):
            at = pl.ds(pl.multiple_of(k * rows, rows), rows)
            sum_ref[at, :] = matmul(left[at, :], right_ref[...]).astype(BF16)
            return c

        lax.fori_loop(0, D // rows, body, 0)

    for k, right_ref in enumerate((gate_ref, up_ref, hidden_ref)):
        pl.when(step // 2 == k)(lambda right_ref=right_ref: product(right_ref))


def weight_sums(normal_mid, grad_out, grad_gate, grad_upward, hidden):
    tokens, width = hidden.shape
    half = width // 2
    whole = pl.BlockSpec((tokens, D), lambda s: (0, 0), pipeline_mode=pl.Buffered(1))

    def columns(first):
        return pl.BlockSpec((tokens, half), lambda s: (0, jnp.clip(s - first, 0, 1)))

    return pl.pallas_call(
        weights_kernel,
        out_shape=jax.ShapeDtypeStruct((D, 3 * width), BF16),
        grid_spec=pltpu.PrefetchScalarGridSpec(
            num_scalar_prefetch=0,
            grid=(6,),
            in_specs=[whole, whole, columns(0), columns(2), columns(4)],
            out_specs=pl.BlockSpec((D, half), lambda s: (0, s)),
            scratch_shapes=[pltpu.VMEM((D, tokens), BF16)],
        ),
        compiler_params=pltpu.CompilerParams(vmem_limit_bytes=48 << 20),
        cost_estimate=pl.CostEstimate(
            flops=6 * tokens * D * width, bytes_accessed=6 * width * (tokens + D), transcendentals=0
        ),
    )(normal_mid, grad_out, grad_gate, grad_upward, hidden)


def pad_to(values, rows, columns):
    return jnp.pad(values, ((0, rows - values.shape[0]), (0, columns - values.shape[1])))


def lanes_up(size):
    return -(-size // LANE) * LANE


class Places:
    def __init__(self, mesh):
        self.sizes = {name: mesh.shape[name] for name in ("row", "col")}
        bits = {name: size.bit_length() - 1 for name, size in self.sizes.items()}
        self.live = [("row", b) for b in reversed(range(bits["row"]))]
        self.live += [("col", b) for b in reversed(range(bits["col"]))]
        rows = [("row", b) for b in range(bits["row"])]
        cols = [("col", b) for b in range(bits["col"])]
        self.first = rows[0]
        self.orders = (rows[1:] + cols, cols[:1] + rows[1:] + cols[1:])

    def mine(self, place):
        return (lax.axis_index(place[0]) >> place[1]) & 1

    def swap(self, values, place):
        axis, bit = place
        pairs = [(i, i ^ (1 << bit)) for i in range(self.sizes[axis])]
        return lax.ppermute(values, axis, pairs)

    def split(self, values, live, place, dim=0):
        pre = 2 ** live.index(place)
        shape = values.shape
        parts = values.reshape(shape[:dim] + (pre, 2, -1) + shape[dim + 1 :])
        half = shape[:dim] + (shape[dim] // 2,) + shape[dim + 1 :]
        mine = self.mine(place)
        send = lax.dynamic_index_in_dim(parts, 1 - mine, dim + 1, keepdims=False)
        keep = lax.dynamic_index_in_dim(parts, mine, dim + 1, keepdims=False)
        return send.reshape(half), keep.reshape(half)


def added(keep, got):
    return keep.astype(F32) + got.astype(F32)


class Chain:
    def __init__(self, places, values, order):
        self.places = places
        self.keep = values
        self.got = None
        self.live = [place for place in places.live if place != places.first]
        self.order = places.orders[order]
        self.at = 0

    def values(self):
        return self.keep if self.got is None else added(self.keep, self.got)

    def prepare(self):
        place = self.order[self.at]
        send, self.keep = self.places.split(self.values().astype(BF16), self.live, place)
        return send

    def launch(self, send):
        place = self.order[self.at]
        self.got = self.places.swap(send, place)
        self.live = [other for other in self.live if other != place]
        self.at += 1

    def finish(self):
        while self.at < len(self.order):
            self.launch(self.prepare())
        return self.values()


def tick(chains, *values):
    sends = tuple(chain.prepare() for chain in chains)
    held = lax.optimization_barrier((sends, values))
    for chain, send in zip(chains, held[0]):
        chain.launch(send)
    return held[1]


def halves(places, values):
    cut = lanes_up(values.shape[1] // 2)
    return [Chain(places, values[:, :cut], 0), Chain(places, values[:, cut:], 1)]


def joined(chains):
    return jnp.concatenate([chain.finish() for chain in chains], axis=1)


def solution(mesh):
    both = ("row", "col")
    devices = mesh.shape["row"] * mesh.shape["col"]
    places = Places(mesh)

    def shards(
        pixels,
        text,
        token_source,
        example_ids,
        cotangent,
        conv_weight,
        conv_bias,
        proj_weight,
        proj_bias,
        first_gain,
        query_weight,
        key_weight,
        value_weight,
        out_weight,
        second_gain,
        gate_weight,
        up_weight,
        down_weight,
    ):
        pixel_depth = pixels.shape[-1]
        vision, block = proj_weight.shape
        vision_block = conv_weight.shape[1]
        hidden_width = gate_weight.shape[1]
        pixel_lanes = lanes_up(pixel_depth + 1)

        folds = -(-vision_block // block)
        conv_local = jnp.concatenate((conv_weight.T, conv_bias[:, None]), axis=1)
        conv_local = pad_to(conv_local, folds * block, pixel_lanes)
        vectors = jnp.stack((proj_bias, first_gain, second_gain), axis=1)
        pieces = [conv_local[f * block : (f + 1) * block] for f in range(folds)]
        pieces += [proj_weight.T, pad_to(vectors, block, LANE)]
        triple = (query_weight, key_weight, value_weight)
        triple = jnp.stack([part.reshape(block, PAIRS, LANE) for part in triple], axis=2)
        pieces += [triple.reshape(block, 3 * D), out_weight.T]
        front = lax.all_gather(jnp.concatenate(pieces, axis=1), both, axis=0, tiled=True)
        ffn = lax.all_gather(
            jnp.concatenate((gate_weight, up_weight, down_weight.T), axis=1),
            both,
            axis=0,
            tiled=True,
        )
        at = folds * pixel_lanes
        conv_t = front[:, :at].reshape(devices, block, folds, pixel_lanes).transpose(0, 2, 1, 3)
        conv_t = conv_t.reshape(devices, folds * block, pixel_lanes)[:, :vision_block]
        conv_t = conv_t.reshape(devices * vision_block, pixel_lanes)
        proj_t = front[:, at : at + vision]
        at += vision
        vector_rows = front[:, at : at + LANE].T.astype(F32)
        proj_add, gain_first, gain_second = vector_rows[0], vector_rows[1], vector_rows[2]
        at += LANE
        qkv_whole = front[:, at : at + 3 * D]
        out_t = front[:, at + 3 * D :]
        gate_whole = ffn[:, :hidden_width]
        up_whole = ffn[:, hidden_width : 2 * hidden_width]
        down_t = ffn[:, 2 * hidden_width :]

        cells = pixels.reshape(-1, pixel_depth)
        ones = jnp.ones((cells.shape[0], 1), BF16)
        cells = pad_to(jnp.concatenate((cells, ones), axis=1), cells.shape[0], pixel_lanes)
        slots = lax.all_to_all(cells, both, split_axis=0, concat_axis=0, tiled=True)
        source = token_source[:, None]
        is_patch = source < PATCH_SLOTS
        pick_patch = (source == lax.iota(jnp.int32, PATCH_SLOTS)[None, :]).astype(BF16)
        text_ids = lax.iota(jnp.int32, text.shape[0]) + PATCH_SLOTS
        pick_text = (source == text_ids[None, :]).astype(BF16)
        patches = matmul(pick_patch, slots).astype(BF16)
        text_tokens = matmul(pick_text, text).astype(BF16)

        visual = right_contract(patches, conv_t).astype(BF16)
        embedded = (right_contract(visual, proj_t) + proj_add).astype(BF16)
        residual = jnp.where(is_patch, embedded, text_tokens).astype(F32)
        scale_one = lax.rsqrt(jnp.mean(residual * residual, axis=-1, keepdims=True) + 1e-06)
        normal_in = (residual * scale_one * gain_first).astype(BF16)
        qkv = matmul(normal_in, qkv_whole).astype(BF16)
        mixed, logsum = attend(qkv, example_ids)
        middle = residual + right_contract(mixed, out_t)
        scale_two = lax.rsqrt(jnp.mean(middle * middle, axis=-1, keepdims=True) + 1e-06)
        normal_mid = (middle * scale_two * gain_second).astype(BF16)
        gate = matmul(normal_mid, gate_whole)
        upward = matmul(normal_mid, up_whole)
        gate_act, gelu_pull = jax.vjp(gelu_tanh, gate)
        hidden = (gate_act * upward).astype(BF16)
        output = (middle + right_contract(hidden, down_t)).astype(BF16)

        def partial(left, right):
            return left_contract(left, right).astype(BF16)

        def core_split(values):
            return places.split(values, places.live, places.first)

        def core_sum(keep, send):
            return added(keep, places.swap(send, places.first))

        grad_hidden = matmul(cotangent, down_t)
        grad_gate = gelu_pull(grad_hidden * upward)[0].astype(BF16)
        grad_upward = (grad_hidden * gate_act).astype(BF16)
        ffn_sums, grad_gate, grad_upward = lax.optimization_barrier(
            (
                weight_sums(normal_mid, cotangent, grad_gate, grad_upward, hidden),
                grad_gate,
                grad_upward,
            )
        )
        ffn_sums = lax.psum_scatter(ffn_sums, both, scatter_dimension=0, tiled=True).astype(F32)
        grad_mid = right_contract(grad_gate, gate_whole) + right_contract(grad_upward, up_whole)
        gain_two_sum = jnp.sum(grad_mid * middle * scale_two, axis=0)
        pulled = grad_mid * gain_second
        pulled_mean = jnp.mean(pulled * middle, axis=-1, keepdims=True)
        grad_middle = cotangent.astype(F32) + scale_two * (
            pulled - middle * (scale_two * scale_two) * pulled_mean
        )
        grad_branch = grad_middle.astype(BF16)

        grad_mixed = matmul(grad_branch, out_t).astype(BF16)
        out_send, out_keep = core_split(partial(grad_branch, mixed))
        out_send, grad_mixed = lax.optimization_barrier((out_send, grad_mixed))
        out_sum = core_sum(out_keep, out_send)
        cut = PAIRS // 2

        def back(grads, start):
            return attend_back(qkv, grads, mixed, logsum, example_ids, start, PAIRS - cut)

        early = back(grad_mixed, 0)
        early_send, early_keep = core_split(partial(normal_in, early))
        early_send, grad_mixed = lax.optimization_barrier((early_send, grad_mixed))
        early_sum = core_sum(early_keep, early_send)
        one = halves(places, jnp.concatenate((early_sum, out_sum), axis=1))
        early, grad_mixed = tick(one, early, grad_mixed)
        late = back(grad_mixed, cut)
        late_send, late_keep = core_split(partial(normal_in, late))
        late_send, late = tick(one, late_send, late)

        at = early.shape[1]
        grad_normal = right_contract(early, qkv_whole[:, :at])
        grad_normal += right_contract(late, qkv_whole[:, at:])
        two = halves(places, core_sum(late_keep, late_send))
        (grad_normal,) = tick(one + two, grad_normal)
        gain_one_sum = jnp.sum(grad_normal * residual * scale_one, axis=0)
        pulled = grad_normal * gain_first
        pulled_mean = jnp.mean(pulled * residual, axis=-1, keepdims=True)
        grad_residual = grad_middle + scale_one * (
            pulled - residual * (scale_one * scale_one) * pulled_mean
        )

        grad_embedded = jnp.where(is_patch, grad_residual, 0.0).astype(BF16)
        (grad_embedded,) = tick(one + two, grad_embedded)
        grad_visual = matmul(grad_embedded, proj_t).astype(BF16)
        grad_patches = matmul(grad_visual, conv_t).astype(BF16)
        slot_ids = lax.iota(jnp.int32, PATCH_SLOTS)[:, None]
        named = (slot_ids == token_source[None, :]).astype(BF16)
        grad_slots = matmul(named, grad_patches).astype(BF16)
        grad_slots, grad_visual, grad_embedded = tick(
            two, grad_slots, grad_visual, grad_embedded
        )
        grad_cells = lax.all_to_all(grad_slots, both, split_axis=0, concat_axis=0, tiled=True)
        grad_pixels = grad_cells[:, :pixel_depth].astype(F32).reshape(pixels.shape)
        proj_add_sum = jnp.sum(grad_embedded.astype(F32), axis=0)
        sums = jnp.stack((proj_add_sum, gain_one_sum, gain_two_sum), axis=0)
        sums = pad_to(sums, LANE, D).T.astype(BF16)
        conv_sum = partial(grad_visual, patches)
        proj_sum = partial(grad_embedded, visual)
        conv_sum = conv_sum.reshape(devices, vision_block, pixel_lanes)
        conv_sum = jnp.pad(conv_sum, ((0, 0), (0, folds * block - vision_block), (0, 0)))
        conv_sum = conv_sum.reshape(devices, folds, block, pixel_lanes).transpose(0, 2, 1, 3)
        conv_sum = conv_sum.reshape(D, folds * pixel_lanes)
        three = jnp.concatenate((proj_sum, sums, conv_sum), axis=1)
        three_send, three_keep = core_split(three)
        tick(two)
        three = halves(places, core_sum(three_keep, three_send))
        tick(three)
        others = one + two
        kept = tick(three, *[chain.keep for chain in others])
        for chain, keep in zip(others, kept):
            chain.keep = keep
        three = joined(three)
        one, two = joined(one), joined(two)
        at = early_sum.shape[1]
        grad_qkv = jnp.concatenate((one[:, :at], two), axis=1).reshape(block, PAIRS, 3, LANE)
        grad_query, grad_key, grad_value = [
            grad_qkv[:, :, k].reshape(block, D) for k in range(3)
        ]
        grad_proj_t, sums = three[:, :vision], three[:, vision : vision + LANE]
        grad_conv_t = three[:, vision + LANE :].reshape(block, folds, pixel_lanes)
        grad_conv_t = grad_conv_t.transpose(1, 0, 2).reshape(folds * block, pixel_lanes)
        grad_conv_t = grad_conv_t[:vision_block]
        return (
            output,
            grad_pixels,
            grad_conv_t[:, :pixel_depth].T,
            grad_conv_t[:, pixel_depth],
            grad_proj_t.T,
            sums[:, 0],
            sums[:, 1],
            grad_query,
            grad_key,
            grad_value,
            one[:, at:].T,
            sums[:, 2],
            ffn_sums[:, :hidden_width],
            ffn_sums[:, hidden_width : 2 * hidden_width],
            ffn_sums[:, 2 * hidden_width :].T,
        )

    rows = P(both, None)
    columns = P(None, both)
    vector = P(both)
    tiles = P("row", "col", None)

    return jax.shard_map(
        shards,
        mesh=mesh,
        in_specs=(
            tiles,
            rows,
            vector,
            vector,
            rows,
            columns,
            vector,
            columns,
            vector,
            vector,
            rows,
            rows,
            rows,
            columns,
            vector,
            rows,
            rows,
            columns,
        ),
        out_specs=(
            rows,
            tiles,
            columns,
            vector,
            columns,
            vector,
            vector,
            rows,
            rows,
            rows,
            columns,
            vector,
            rows,
            rows,
            columns,
        ),
        check_vma=False,
    )
```
